32 devices in a mesh: flow: 4 (over z), width: 8 (over y, x, core).
Axes of the slice: x: 2, y: 2, z: 4, core: 2. Of those that a mesh axis runs over, the one named last changes fastest.
Arguments:
- positions: float32 [3, 262144], P(None, ('flow', 'width')), may hold values from -0.5 to 0.5
- vorticity: float32 [3, 262144], P(None, ('flow', 'width')), may hold values from -6 to 6
- dest_slot: int32 [262144], P(('flow', 'width')), may hold values from 0 to 8191, as said below
- send_counts: int32 [32, 8], P(('flow', 'width')), may hold values from 256 to 1024, as said below
- near_pairs: int32 [16, 128, 3], P('flow', 'width'), may hold values from 0 to 7, as said below
- box_top: int32 [16, 128], P('flow', 'width'), may hold values from 0 to 1023
- box_offset: float32 [3, 16, 128], P(None, 'flow', 'width'), may hold values from -2 to 2
Outputs:
- velocity: float32 [3, 16, 128, 128], P(None, 'flow', 'width')
- moments: float32 [8, 1024, 495], P('width', 'flow')
The draws below stay inside these ranges and needn't reach their ends.
Inputs may be any that keep to these rules, and one draw needn't show every extreme that they name: `send_counts`: entry r of row f * 8 + s counts the live send slots of sender (f, s) for receiver r; in every flow row one receiver gets 1024 from every sender. `dest_slot`: among the live send slots bound for one receiver the values are distinct; values in slots that are not live are arbitrary. `near_pairs`: the 3 codes of a box are distinct.
All inputs are finite; a program needn't handle non-finite values.
Results may differ from the reference program's by a relative error of at most 0.0003.
Values sent between devices are 32-bit elements; how exact they have to be, the bound alone decides.
No kernel may reach another device: no remote copies, remote signals or barrier semaphores. Data moves between devices by JAX's collectives and lax.ppermute only.
A program may use at most 64 MiB of HBM per device.

```python
import math
import jax
import jax.numpy as jnp
from jax import lax

BX = 4
BY = 16
SLOT = 128
NEAR = 3
ORDER = 8
TOP = 1024
COEF = 495
BOX_SLOTS = 8192
CAP = 1024
GF = 16
GW = 128
TOTAL = 262144
N_FLOW = 4
N_WIDTH = 8


def shuffle_slots(slot_key):
    return jax.random.permutation(slot_key, BOX_SLOTS)


def routing_tables(key):
    base_key = jax.random.fold_in(key, 7001)
    full_key, count_key, slot_key, junk_key = jax.random.split(base_key, 4)
    full_receiver = jax.random.randint(full_key, (N_FLOW, 1, 1), 0, N_WIDTH)
    drawn_counts = jax.random.randint(count_key, (N_FLOW, N_WIDTH, N_WIDTH), CAP // 4, CAP + 1)
    receivers = jnp.arange(N_WIDTH, dtype=jnp.int32)[None, None, :]
    counts = jnp.where(receivers == full_receiver, CAP, drawn_counts).astype(jnp.int32)
    live_slots = jnp.arange(CAP, dtype=jnp.int32)[None, None, None, :] < counts[:, :, :, None]
    live_recv = live_slots.transpose(0, 2, 1, 3).reshape(N_FLOW * N_WIDTH, BOX_SLOTS)
    rank_in_box = jnp.cumsum(live_recv.astype(jnp.int32), axis=1) - 1
    perm_keys = jax.random.split(slot_key, N_FLOW * N_WIDTH)
    shuffled = jax.vmap(shuffle_slots)(perm_keys)
    chosen = jnp.take_along_axis(shuffled, jnp.clip(rank_in_box, 0, BOX_SLOTS - 1), axis=1)
    junk_slots = jax.random.randint(junk_key, (N_FLOW * N_WIDTH, BOX_SLOTS), 0, BOX_SLOTS)
    slot_values = jnp.where(live_recv, chosen, junk_slots).astype(jnp.int32)
    slot_values = slot_values.reshape(N_FLOW, N_WIDTH, N_WIDTH, CAP).transpose(0, 2, 1, 3).reshape(TOTAL)
    return (counts.reshape(N_FLOW * N_WIDTH, N_WIDTH), slot_values)


def draw_send_counts(key, part):
    return routing_tables(key)[0]


def draw_dest_slot(key, part):
    return routing_tables(key)[1]


def draw_near_pairs(key, part):
    near_key = jax.random.fold_in(key, 9103)
    scores = jax.random.randint(near_key, (GF, GW, 8), 0, 1 << 20) * 8 + jnp.arange(8, dtype=jnp.int32)
    ordered = jnp.argsort(scores, axis=-1)
    return ordered[:, :, :NEAR].astype(jnp.int32)


def draw_box_offset(key, part):
    offset_key = jax.random.fold_in(key, 4409)
    size_key = jax.random.fold_in(offset_key, 0)
    return jax.random.uniform(size_key, (3, GF, GW), jnp.float32, -2.0, 2.0)


def with_ends(result, rng, smallest, high):
    longest = result.shape.index(max(result.shape))
    spots = []
    for shift in (0, 1):
        where = [jax.random.randint(jax.random.fold_in(rng, axis), (), 0, length) for axis, length in enumerate(result.shape)]
        where[longest] = (where[longest] + shift) % result.shape[longest]
        spots.append(tuple(where))
    return result.at[spots[0]].set(smallest).at[spots[1]].set(high)


def level_of(stream_key, shape, pieces, low, high):
    gain = 1.0
    for dim, parts in pieces:
        steps = jax.random.uniform(jax.random.fold_in(jax.random.fold_in(stream_key, 6), dim), (parts,), jnp.float32, low / len(pieces), high / len(pieces))
        gain = gain * jnp.repeat(jnp.exp(steps), shape[dim] // parts).reshape((-1,) + (1,) * (len(shape) - 1 - dim))
    return gain


def noise(stream_key, dims, scale, bound, cuts=(), kind=jnp.bfloat16):
    loudness = level_of(stream_key, dims, cuts, -0.22, 0.18) if cuts else 1.0
    entries = jax.random.normal(stream_key, dims, jnp.float32) * scale * loudness
    return jnp.minimum(jnp.maximum(entries, -bound), bound).astype(kind)


def setup_inputs(seed: int = 0) -> dict:
    streams_of = jax.random.split(jax.random.key(seed), 8)
    positions = jnp.clip(jax.random.uniform(streams_of[0], (3, TOTAL), jnp.float32, -0.5, 0.5) * level_of(streams_of[0], (3, TOTAL), ((1, 32),), -0.4, 0.0), -0.5, 0.5)
    vorticity = noise(streams_of[1], (3, TOTAL), 1.0, 6.0, ((1, 32),), jnp.float32)
    dest_slot = draw_dest_slot(jax.random.fold_in(streams_of[7], 71), 0)
    send_counts = draw_send_counts(jax.random.fold_in(streams_of[7], 71), 0)
    near_pairs = draw_near_pairs(jax.random.fold_in(streams_of[7], 71), 0)
    box_top = with_ends(jax.random.randint(streams_of[5], (GF, GW), 0, TOP), jax.random.fold_in(streams_of[5], 1), 0, TOP - 1).astype(jnp.int32)
    box_offset = draw_box_offset(jax.random.fold_in(streams_of[7], 71), 0)
    return dict(positions=positions, vorticity=vorticity, dest_slot=dest_slot, send_counts=send_counts, near_pairs=near_pairs, box_top=box_top, box_offset=box_offset)


core_sq = 0.25
inv_four_pi = 0.07957747154594767
row_steps = (-1, -1, -1, 0, 0, 1, 1, 1)
col_steps = (-1, 0, 1, -1, 1, -1, 0, 1)
highest = lax.Precision.HIGHEST

def monomials(relative):
    powers = []
    for axis_number in range(3):
        column = [jnp.ones_like(relative[axis_number])]
        for degree in range(ORDER):
            column.append(column[-1] * relative[axis_number])
        powers.append(column)
    term_list = []
    for degree_sum in range(ORDER + 1):
        for power_a in range(degree_sum, -1, -1):
            for power_b in range(degree_sum - power_a, -1, -1):
                power_c = degree_sum - power_a - power_b
                inverse_factor = 1.0 / (math.factorial(power_a) * math.factorial(power_b) * math.factorial(power_c))
                term_list.append(powers[0][power_a] * powers[1][power_b] * powers[2][power_c] * inverse_factor)
    return jnp.stack(term_list)

def pair_sums(targets, source, shift_row, shift_col):
    src_x = source[0] + shift_row[:, None]
    src_y = source[1] + shift_col[:, None]
    src_z = source[2]
    spin_x, spin_y, spin_z = (source[3], source[4], source[5])
    delta_x = targets[0][:, :, None] - src_x[:, None, :]
    delta_y = targets[1][:, :, None] - src_y[:, None, :]
    delta_z = targets[2][:, :, None] - src_z[:, None, :]
    dist_sq = delta_x * delta_x + delta_y * delta_y + delta_z * delta_z + core_sq
    kernel = 1.0 / (dist_sq * jnp.sqrt(dist_sq))
    weighted_in = jnp.stack([spin_x, spin_y, spin_z, src_y * spin_z - src_z * spin_y, src_z * spin_x - src_x * spin_z, src_x * spin_y - src_y * spin_x])
    return jnp.einsum('bij,fbj->fbi', kernel, weighted_in, precision=highest)

def row_work(window, code_block, occupied_block, offset_block):
    count_boxes = code_block.shape[0]
    targets = window[:, 1, 1:count_boxes + 1]
    stacked = jnp.stack([window[:, 1 + row_steps[code_index], 1 + col_steps[code_index]:1 + col_steps[code_index] + count_boxes] for code_index in range(8)])
    zero_shift = jnp.zeros((count_boxes,), jnp.float32)
    totals = pair_sums(targets, targets, zero_shift, zero_shift)
    row_table = jnp.array(row_steps, jnp.float32)
    col_table = jnp.array(col_steps, jnp.float32)
    for listed in range(code_block.shape[1]):
        selector = (code_block[:, listed][:, None] == jnp.arange(8, dtype=jnp.int32)[None, :]).astype(jnp.float32)
        source = jnp.einsum('bc,cfbs->fbs', selector, stacked, precision=highest)
        shift_row = jnp.einsum('bc,c->b', selector, row_table, precision=highest)
        shift_col = jnp.einsum('bc,c->b', selector, col_table, precision=highest)
        totals = totals + pair_sums(targets, source, shift_row, shift_col)
    cross_x = targets[1] * totals[2] - targets[2] * totals[1]
    cross_y = targets[2] * totals[0] - targets[0] * totals[2]
    cross_z = targets[0] * totals[1] - targets[1] * totals[0]
    velocity = -inv_four_pi * occupied_block[None] * (jnp.stack([cross_x, cross_y, cross_z]) - totals[3:6])
    relative = targets[0:3] + offset_block[:, :, None]
    basis_terms = monomials(relative)
    moments = jnp.einsum('mbs,cbs->bcm', basis_terms, targets[3:6], precision=highest)
    return (velocity, moments.reshape(count_boxes, 3 * basis_terms.shape[0]))

def place_records(records, slot_list):
    return jnp.zeros((6, BOX_SLOTS), jnp.float32).at[:, slot_list].set(records, mode='drop')

def mark_slots(slot_list):
    return jnp.zeros((BOX_SLOTS,), jnp.float32).at[slot_list].set(1.0, mode='drop')

def column_tops(values, top_list):
    return jax.ops.segment_sum(values, top_list, num_segments=TOP)

def reference(positions, vorticity, dest_slot, send_counts, near_pairs, box_top, box_offset):
    records = jnp.concatenate([positions, vorticity], axis=0)
    records = records.reshape(6, N_FLOW, N_WIDTH, N_WIDTH, CAP).transpose(0, 1, 3, 2, 4).reshape(6, N_FLOW * N_WIDTH, BOX_SLOTS)
    counts = send_counts.reshape(N_FLOW, N_WIDTH, N_WIDTH)
    live_slots = jnp.arange(CAP, dtype=jnp.int32)[None, None, None, :] < counts[:, :, :, None]
    slot_lists = jnp.where(live_slots, dest_slot.reshape(N_FLOW, N_WIDTH, N_WIDTH, CAP), BOX_SLOTS).astype(jnp.int32)
    slot_lists = slot_lists.transpose(0, 2, 1, 3).reshape(N_FLOW * N_WIDTH, BOX_SLOTS)
    placed = jax.vmap(place_records, in_axes=(1, 0))(records, slot_lists)
    marked = jax.vmap(mark_slots)(slot_lists)
    box_records = placed.reshape(N_FLOW, N_WIDTH, 6, BX, BY, SLOT).transpose(2, 0, 3, 1, 4, 5).reshape(6, GF, GW, SLOT)
    occupied = marked.reshape(N_FLOW, N_WIDTH, BX, BY, SLOT).transpose(0, 2, 1, 3, 4).reshape(GF, GW, SLOT)
    padded = jnp.pad(box_records, ((0, 0), (1, 1), (1, 1), (0, 0)))
    offset_rows = box_offset.transpose(1, 0, 2)

    def one_row(inputs):
        row_index, code_block, occupied_block, offset_block = inputs
        window = lax.dynamic_slice_in_dim(padded, row_index, 3, axis=1)
        return row_work(window, code_block, occupied_block, offset_block)
    velocity, moments = lax.map(one_row, (jnp.arange(GF, dtype=jnp.int32), near_pairs, occupied, offset_rows))
    velocity = velocity.transpose(1, 0, 2, 3)
    column_moments = moments.reshape(GF, N_WIDTH, BY, COEF).transpose(1, 0, 2, 3).reshape(N_WIDTH, GF * BY, COEF)
    column_ids = box_top.reshape(GF, N_WIDTH, BY).transpose(1, 0, 2).reshape(N_WIDTH, GF * BY).astype(jnp.int32)
    summed = jax.vmap(column_tops)(column_moments, column_ids)
    return (velocity, summed)
```

```python
import functools
import math

import jax
import jax.numpy as jnp
from jax import lax
from jax.experimental import pallas as pl
from jax.experimental.pallas import tpu as pltpu
from jax.sharding import PartitionSpec as P

SLOT = 128
ORDER = 8
TOP = 1024
TERMS = [
    (a, b, s - a - b)
    for s in range(ORDER + 1)
    for a in range(s, -1, -1)
    for b in range(s - a, -1, -1)
]
N_TERMS = len(TERMS)
COEF = 3 * N_TERMS
HALF_ROWS = (COEF + 1) // 2
LAG = 2
UNROLL = 16
LOW = 256

core_sq = 0.25
inv_four_pi = 0.07957747154594767
f32 = jnp.float32
bf16 = jnp.bfloat16
VMEM = pltpu.VMEM
SMEM = pltpu.SMEM


def split2(x):
    high = x.astype(bf16).astype(f32)
    return high, x - high


def rows8(x_shape=(8, SLOT)):
    return lax.broadcasted_iota(jnp.int32, x_shape, 0)


def pack_kernel(counts, positions, vorticity, dest, *refs):
    *outs, pos, vor, ids, sems = refs
    copies = [
        pltpu.make_async_copy(src, dst, sems.at[n])
        for n, (src, dst) in enumerate([(positions, pos), (vorticity, vor), (dest, ids)])
    ]
    for copy in copies:
        copy.start()
    peers = len(outs)
    per_peer = outs[0].shape[1]
    total = pos.shape[1]
    lane = lax.broadcasted_iota(jnp.int32, (1, per_peer), 1)
    me = lax.axis_index("width")
    for copy in copies:
        copy.wait()
    for s, out in enumerate(outs):
        r = me ^ s
        part = pl.ds(pl.multiple_of(r * per_peer, SLOT), per_peer)
        out[0:3] = pos[:, part]
        out[3:6] = vor[:, part]
        out[6:7] = jnp.where(lane < counts[0, r], ids[:, part], total).astype(f32)
        out[7:8] = jnp.zeros((1, per_peer), f32)


def scatter_kernel(*refs):
    *arrived, boxes, row_a, row_b, left, right, acc = refs
    per_peer = arrived[0].shape[1]
    highs = acc.shape[0] // 16
    row = lax.broadcasted_iota(jnp.int32, (8, per_peer), 0)
    low_index = lax.broadcasted_iota(jnp.int32, (LOW, per_peer), 0).astype(f32).astype(bf16)
    for s, chunk in enumerate(arrived):
        records = chunk[...]
        ids = records[6:7]
        id_high = jnp.floor(ids * (1.0 / LOW))
        id_low = ids - id_high * LOW
        kept = jnp.where(row == 6, 1.0, records)
        high, low = split2(kept)
        pieces = jnp.concatenate([high, low], axis=0).astype(bf16)
        high_b = jnp.broadcast_to(id_high, (16, per_peer)).astype(bf16)
        zero = jnp.zeros_like(pieces)
        lhs = jnp.concatenate(
            [jnp.where(high_b == jnp.asarray(h, bf16), pieces, zero) for h in range(highs)], axis=0
        )
        low_b = jnp.broadcast_to(id_low, (LOW, per_peer)).astype(bf16)
        rhs = jnp.where(low_b == low_index, jnp.ones((), bf16), jnp.zeros((), bf16))
        term = lax.dot_general(lhs, rhs, (((1,), (1,)), ((), ())), preferred_element_type=f32)
        if s == 0:
            acc[...] = term
        else:
            acc[...] += term
    rows_here, cols_here = boxes.shape[:2]
    for h in range(highs):
        block = acc[16 * h : 16 * h + 8] + acc[16 * h + 8 : 16 * h + 16]
        for k in range(LOW // SLOT):
            i, j = divmod(h * (LOW // SLOT) + k, cols_here)
            piece = block[:, k * SLOT : (k + 1) * SLOT]
            boxes[i, j] = piece
            if j == 0:
                left[i] = piece
            if j == cols_here - 1:
                right[i] = piece
    even = (lax.axis_index("flow") & 1) == 0
    row_a[...] = jnp.where(even, boxes[rows_here - 1], boxes[0])
    row_b[...] = jnp.where(even, boxes[0], boxes[rows_here - 1])


def moments_kernel(offset, tops, boxes, out, moved, acc):
    rows_here, cols_here = boxes.shape[:2]
    count = rows_here * cols_here
    row = rows8()
    for b in range(count):
        i, j = divmod(b, cols_here)
        add = jnp.where(
            row == 0,
            offset[0, i, j],
            jnp.where(row == 1, offset[1, i, j], jnp.where(row == 2, offset[2, i, j], 0.0)),
        )
        moved[8 * b : 8 * b + 8] = boxes[i, j] + add
    fields = []
    for f in range(6):
        plane = moved[pl.ds(f, count, stride=8), :]
        both = jnp.concatenate([plane, pltpu.roll(plane, SLOT - count, 1)], axis=0)
        fields.append(jnp.transpose(both)[:count])
    chunk = 16
    for k in range(count // chunk):
        part = slice(k * chunk, (k + 1) * chunk)
        powers = []
        for f in range(3):
            x = fields[f][part]
            column = [None, x]
            for d in range(2, ORDER + 1):
                column.append(column[-1] * (x * (1.0 / d)))
            powers.append(column)
        spins = [fields[3 + f][part] for f in range(3)]
        index = {t: m for m, t in enumerate(TERMS)}
        for a in range(ORDER + 1):
            lead_a = spins if a == 0 else [w * powers[0][a] for w in spins]
            for b in range(ORDER + 1 - a):
                lead = lead_a if b == 0 else [w * powers[1][b] for w in lead_a]
                for n in range(ORDER + 1 - a - b):
                    m = index[(a, b, n)]
                    for c in range(3):
                        value = lead[c] if n == 0 else lead[c] * powers[2][n]
                        value = value[:8] + value[8:]
                        at = c * N_TERMS + m
                        if k == 0:
                            acc[8 * at : 8 * at + 8] = value
                        else:
                            acc[8 * at : 8 * at + 8] += value
    acc[8 * COEF : 8 * COEF + 8] = jnp.zeros((8, SLOT), f32)
    total = acc[pl.ds(0, 2 * HALF_ROWS, stride=8), :]
    for s in range(1, 8):
        total = total + acc[pl.ds(s, 2 * HALF_ROWS, stride=8), :]
    total = total + pltpu.roll(total, count, 1)
    lane = lax.broadcasted_iota(jnp.int32, (HALF_ROWS, SLOT), 1)
    out[...] = jnp.where(lane < count, total[:HALF_ROWS], total[HALF_ROWS:])
    lane1 = lax.broadcasted_iota(jnp.int32, (1, SLOT), 1)
    top_row = out[HALF_ROWS - 1 : HALF_ROWS, :]
    for b in range(count):
        i, j = divmod(b, cols_here)
        top_row = jnp.where(lane1 == count + b, tops[i, j].astype(f32), top_row)
    out[HALF_ROWS - 1 : HALF_ROWS, :] = top_row


def tops_kernel(*refs):
    *shares, out = refs
    parts = out.shape[0] // COEF
    tops_here = parts * out.shape[1]
    base = lax.axis_index("flow") * tops_here
    lane = lax.broadcasted_iota(jnp.int32, (HALF_ROWS, SLOT), 1)
    wanted = (lax.broadcasted_iota(jnp.int32, (tops_here, SLOT), 0) + base).astype(f32)
    half = SLOT // 2
    total = None
    for f in range(0, len(shares), 2):
        one, two = shares[f][...], shares[f + 1][...]
        upper = jnp.where(lane < half, one, pltpu.roll(two, half, 1))
        lower = jnp.where(lane < half, pltpu.roll(one, half, 1), two)
        member = jnp.where(wanted == lower[HALF_ROWS - 1 : HALF_ROWS], 1.0, 0.0).astype(bf16)
        rest = jnp.concatenate([upper, lower], axis=0)
        for _ in range(3):
            piece = rest.astype(bf16)
            rest = rest - piece.astype(f32)
            term = lax.dot_general(
                piece, member, (((1,), (1,)), ((), ())), preferred_element_type=f32
            )
            total = term if total is None else total + term
    if parts == 1:
        out[...] = total[:COEF]
    else:
        for k in range(parts):
            out[pl.ds(k, COEF, stride=parts), :] = total[:COEF, k * SLOT : (k + 1) * SLOT]


def near_kernel(
    pairs, center, row_a, row_b, col_a, col_b, out, pad, feat, target, raw, weight, shifts, masks, k_high, k_low, sums
):
    rows_here, cols_here = center.shape[:2]
    count = rows_here * cols_here
    wide = cols_here + 2
    boxes_all = (rows_here + 2) * wide
    row = rows8()

    def at8(b):
        return pl.ds(b * 8 if isinstance(b, int) else pl.multiple_of(b * 8, 8), 8)

    def field_of(ref, first, f):
        return ref[pl.ds(first * 8 + f, 8, stride=8), :]

    even_f = (lax.axis_index("flow") & 1) == 0
    even_w = (lax.axis_index("width") & 1) == 0
    for j in range(cols_here):
        for i in range(rows_here):
            pad[at8((i + 1) * wide + 1 + j), :] = center[i, j]
        pad[at8(1 + j), :] = jnp.where(even_f, row_b[j], row_a[j])
        pad[at8((rows_here + 1) * wide + 1 + j), :] = jnp.where(even_f, row_a[j], row_b[j])
    for i in range(rows_here + 2):
        pad[at8(i * wide), :] = jnp.where(even_w, col_b[i], col_a[i])
        pad[at8(i * wide + wide - 1), :] = jnp.where(even_w, col_a[i], col_b[i])
    zeros8 = jnp.zeros((8, SLOT), f32)
    for b in range(boxes_all, pad.shape[0] // 8):
        pad[at8(b), :] = zeros8

    for k in range(9):
        d0, d1 = float(k // 3 - 1), float(k % 3 - 1)
        a_rows = [-d0, -d1, 0.0, -d0, -d1, 0.0, d0 * d0 + d1 * d1, 0.0]
        b_rows = [-2 * d0, -2 * d1, 0.0, -2 * d0, -2 * d1, 0.0, 1.0, 1.0]
        tile_a, tile_b = zeros8, zeros8
        for r in range(8):
            tile_a = jnp.where(row == r, a_rows[r], tile_a)
            tile_b = jnp.where(row == r, b_rows[r], tile_b)
        shifts[k] = jnp.concatenate([tile_a, tile_b], axis=0).astype(bf16)
        turns = jnp.zeros((8, SLOT), f32)
        for r, value in enumerate((d1, d0, d0, d1)):
            turns = jnp.where(row == r, value, turns)
        masks[k] = jnp.concatenate([zeros8 + 1.0, turns] * 2, axis=0).astype(bf16)

    for start in range(0, boxes_all, 8):
        y0, y1, y2, w0, w1, w2 = (field_of(pad, start, f) for f in range(6))
        values = [w0, w1, w2, y1 * w2 - y2 * w1, y2 * w0 - y0 * w2, y0 * w1 - y1 * w0, zeros8, zeros8]
        values += [w2, w2, w1, w0] + [zeros8] * 4
        for f, value in enumerate(values):
            raw[pl.ds(start * 16 + f, 8, stride=16), :] = value
        pad[pl.ds(start * 8 + 7, 8, stride=8), :] = y0 * y0 + y1 * y1 + y2 * y2

    def prepare(at, _):
        y = pad[at8(at), :]
        norm = jnp.broadcast_to(y[7:8], (8, SLOT))
        high, low = split2(y)
        turned = pltpu.roll(low, 3, 0)
        n1, rest = split2(norm)
        n2, rest = split2(rest)
        first = jnp.where(row < 3, -2.0 * high, jnp.where(row < 6, -2.0 * turned, 1.0))
        second = jnp.where(row == 7, n1, first)
        fourth = jnp.where(row == 6, n2, jnp.where(row == 7, rest, 1.0))
        feat[at, 0:16] = jnp.concatenate([first, second], axis=0).astype(bf16)
        feat[at, 16:32] = jnp.concatenate([first, fourth], axis=0).astype(bf16)
        high, low = split2(raw[pl.ds(pl.multiple_of(at * 16, 16), 16), :])
        weight[at] = jnp.concatenate([high, low], axis=0).astype(bf16)
        return 0

    lax.fori_loop(0, boxes_all, prepare, 0, unroll=6)

    const_row = jnp.where((row == 2) | (row == 5) | (row == 7), 0.0, 1.0)

    def place(b):
        i = lax.div(b, cols_here) if cols_here & (cols_here - 1) else b >> (cols_here.bit_length() - 1)
        return i, b - i * cols_here

    def sources(b):
        i, j = place(b)
        corner = i * wide + j
        found = [(4, None, None, corner + wide + 1)]
        for q in range(pairs.shape[0]):
            code = pairs[q, i, j]
            k = jnp.where(code >= 4, code + 1, code)
            r = (k * 11) >> 5
            c = k - 3 * r
            found.append((k, r, c, corner + r * wide + c))
        return found

    def target_stage(b, slot):
        i, j = place(b)
        x = pad[at8((i + 1) * wide + 1 + j), :]
        high, low = split2(x)
        a1, rest = split2(jnp.broadcast_to(x[7:8], (8, SLOT)) + core_sq)
        a2, a3 = split2(rest)
        high3, low3 = pltpu.roll(high, 3, 0), pltpu.roll(low, 3, 0)
        rows = [
            jnp.where(row < 3, high, jnp.where(row < 6, high3, jnp.where(row == 6, a1, a2))),
            jnp.where(row < 3, low, jnp.where(row < 6, low3, jnp.where(row == 6, a3, 1.0))),
            const_row,
            jnp.where(row < 3, high, jnp.where(row < 6, low3, 1.0)),
        ]
        target[slot] = jnp.transpose(jnp.concatenate(rows, axis=0).astype(bf16))

    def kernel_stage(b, slot):
        features = []
        for k, _, _, source in sources(b):
            second = feat[source, 16:32] * shifts[k]
            features.append(jnp.concatenate([feat[source, 0:16], second], axis=0))
        feature = jnp.concatenate(features, axis=1)
        dist = lax.dot_general(
            target[slot], feature, (((1,), (0,)), ((), ())), preferred_element_type=f32
        )
        root = lax.rsqrt(dist)
        kernel = root * root * root
        high = kernel.astype(bf16)
        k_high[slot] = high
        k_low[slot] = (kernel - high.astype(f32)).astype(bf16)

    def field_stage(b, slot):
        tiles = [weight[source] * masks[k] for k, _, _, source in sources(b)]
        lhs = jnp.concatenate(tiles, axis=1)
        dims = (((1,), (1,)), ((), ()))
        main = lax.dot_general(lhs, k_high[slot], dims, preferred_element_type=f32)
        rest = lax.dot_general(lhs[0:16], k_low[slot], dims, preferred_element_type=f32)
        sums[0, at8(b), :] = main[0:8] + main[16:24] + rest[0:8]
        sums[1, at8(b), :] = main[8:16] + main[24:32] + rest[8:16]

    slots = k_high.shape[0]
    for u in range(LAG + 1):
        target_stage(u, u)
    for u in range(LAG):
        kernel_stage(u, u)

    def some_boxes(t, _):
        for u in range(slots):
            b = slots * t + u
            kernel_stage(jnp.minimum(b + LAG, count - 1), (u + LAG) % slots)
            field_stage(b, u)
            target_stage(jnp.minimum(b + LAG + 1, count - 1), (u + LAG + 1) % slots)
        return 0

    lax.fori_loop(0, count // slots, some_boxes, 0)

    for i in range(rows_here):
        for j in range(0, cols_here, 8):
            at = (i + 1) * wide + 1 + j
            b = i * cols_here + j
            x0, x1, x2 = (field_of(pad, at, f) for f in range(3))
            scale = -inv_four_pi * field_of(pad, at, 6)
            a0, a1, a2, b0, b1, b2 = (field_of(sums.at[0], b, f) for f in range(6))
            h0, h1, h2, h3 = (field_of(sums.at[1], b, f) for f in range(4))
            out[0, i, j : j + 8, :] = scale * (x1 * a2 - x2 * a1 - (b0 + h0))
            out[1, i, j : j + 8, :] = scale * (x2 * a0 - x0 * a2 - (b1 - h1))
            out[2, i, j : j + 8, :] = scale * (x0 * a1 - x1 * a0 - (b2 + h2 - h3))


def spec(space):
    return pl.BlockSpec(memory_space=space)


def call(kernel, out_shape, spaces, scratch=(), cost=(0, 0), name=None, limit=8):
    many = isinstance(out_shape, (list, tuple))
    return pl.pallas_call(
        kernel,
        out_shape=out_shape,
        in_specs=[spec(s) for s in spaces],
        out_specs=[spec(VMEM)] * len(out_shape) if many else spec(VMEM),
        scratch_shapes=list(scratch),
        compiler_params=pltpu.CompilerParams(vmem_limit_bytes=limit * 1024 * 1024),
        cost_estimate=pl.CostEstimate(flops=cost[0], bytes_accessed=cost[1], transcendentals=0),
        name=name,
    )


def shape(*dims):
    return jax.ShapeDtypeStruct(dims, f32)


def swap(axis, step):
    return [(i, i ^ step) for i in range(lax.axis_size(axis))]


def swap_odd(axis):
    odd = range(1, lax.axis_size(axis) - 1, 2)
    return [(i, i + 1) for i in odd] + [(i + 1, i) for i in odd]


def shards(positions, vorticity, dest_slot, send_counts, near_pairs, box_top, box_offset):
    slot_total = positions.shape[1]
    peers = lax.axis_size("width")
    flows = lax.axis_size("flow")
    per_peer = slot_total // peers
    rows_here, cols_here = box_top.shape
    count = rows_here * cols_here
    outgoing = call(
        pack_kernel,
        [shape(8, per_peer)] * peers,
        [SMEM, pltpu.HBM, pltpu.HBM, pltpu.HBM],
        [
            VMEM((3, slot_total), f32),
            VMEM((3, slot_total), f32),
            VMEM((1, slot_total), jnp.int32),
            pltpu.SemaphoreType.DMA((3,)),
        ],
        name="pack",
        limit=60,
    )(send_counts, positions, vorticity, dest_slot.reshape(1, slot_total))
    arrived = [
        lax.ppermute(outgoing[s], "width", swap("width", s)) for s in range(peers - 1, 0, -1)
    ]
    arrived.append(outgoing[0])
    boxes, row_a, row_b, left, right = call(
        scatter_kernel,
        [shape(rows_here, cols_here, 8, SLOT)]
        + [shape(cols_here, 8, SLOT)] * 2
        + [shape(rows_here, 8, SLOT)] * 2,
        [VMEM] * peers,
        [VMEM((slot_total // LOW * 16, LOW), f32)],
        name="scatter",
    )(*arrived)
    row_a = lax.ppermute(row_a, "flow", swap("flow", 1))
    row_b = lax.ppermute(row_b, "flow", swap_odd("flow"))
    local = call(
        moments_kernel,
        shape(HALF_ROWS, SLOT),
        [SMEM, SMEM, VMEM],
        [VMEM((8 * count, SLOT), f32), VMEM((16 * HALF_ROWS, SLOT), f32)],
        cost=(10_000_000, 1_000_000),
        name="moments",
    )(box_offset, box_top, boxes)
    even_f = (lax.axis_index("flow") & 1) == 0
    even_w = (lax.axis_index("width") & 1) == 0
    up = jnp.where(even_f, row_b, row_a)
    down = jnp.where(even_f, row_a, row_b)
    left = jnp.concatenate([up[:1], left, down[:1]], axis=0)
    right = jnp.concatenate([up[cols_here - 1 :], right, down[cols_here - 1 :]], axis=0)
    left, right, local = lax.optimization_barrier((left, right, local))
    col_a = lax.ppermute(jnp.where(even_w, right, left), "width", swap("width", 1))
    col_b = lax.ppermute(jnp.where(even_w, left, right), "width", swap_odd("width"))
    shares = [lax.ppermute(local, "flow", swap("flow", s)) for s in range(flows - 1, 0, -1)]
    shares.append(local)
    padded = -(-(rows_here + 2) * (cols_here + 2) // 8) * 8
    velocity = call(
        near_kernel,
        shape(3, rows_here, cols_here, SLOT),
        [SMEM] + [VMEM] * 5,
        [
            VMEM((8 * padded, SLOT), f32),
            VMEM((padded, 32, SLOT), bf16),
            VMEM((UNROLL, SLOT, 32), bf16),
            VMEM((16 * padded, SLOT), f32),
            VMEM((padded, 32, SLOT), bf16),
            VMEM((9, 16, SLOT), bf16),
            VMEM((9, 32, SLOT), bf16),
            VMEM((UNROLL, SLOT, 4 * SLOT), bf16),
            VMEM((UNROLL, SLOT, 4 * SLOT), bf16),
            VMEM((2, 8 * count, SLOT), f32),
        ],
        cost=(5_000_000_000, 2_000_000),
        name="near",
        limit=20,
    )(near_pairs.transpose(2, 0, 1), boxes, row_a, row_b, col_a, col_b)
    tops_here = TOP // flows
    parts = max(1, tops_here // SLOT)
    summed = call(tops_kernel, shape(COEF * parts, tops_here // parts), [VMEM] * flows, name="tops")(
        *shares
    )
    return (velocity, summed.reshape(COEF, 1, tops_here).transpose(1, 2, 0))


def solution(mesh):
    placed = (
        P(None, ("flow", "width")),
        P(None, ("flow", "width")),
        P(("flow", "width")),
        P(("flow", "width"), None),
        P("flow", "width", None),
        P("flow", "width"),
        P(None, "flow", "width"),
    )
    return jax.shard_map(
        shards,
        mesh=mesh,
        in_specs=placed,
        out_specs=(P(None, "flow", "width", None), P("width", "flow", None)),
        check_vma=False,
    )
```

```python
import functools
import math

import jax
import jax.numpy as jnp
from jax import lax
from jax.experimental import pallas as pl
from jax.experimental.pallas import tpu as pltpu
from jax.sharding import PartitionSpec as P

SLOT = 128
ORDER = 8
TOP = 1024
TERMS = [
    (a, b, s - a - b)
    for s in range(ORDER + 1)
    for a in range(s, -1, -1)
    for b in range(s - a, -1, -1)
]
N_TERMS = len(TERMS)
COEF = 3 * N_TERMS
HALF_ROWS = (COEF + 1) // 2
LAG = 2
MOMENT_ROWS = 16
UNROLL = 32
LOW = 256

core_sq = 0.25
inv_four_pi = 0.07957747154594767
f32 = jnp.float32
bf16 = jnp.bfloat16
VMEM = pltpu.VMEM
SMEM = pltpu.SMEM


def split2(x):
    high = x.astype(bf16).astype(f32)
    return high, x - high


def rows8(x_shape=(8, SLOT)):
    return lax.broadcasted_iota(jnp.int32, x_shape, 0)


def pack_kernel(counts, positions, vorticity, dest, *refs):
    *outs, pos, vor, ids, sems = refs
    copies = [
        pltpu.make_async_copy(src, dst, sems.at[n])
        for n, (src, dst) in enumerate([(positions, pos), (vorticity, vor), (dest, ids)])
    ]
    for copy in copies:
        copy.start()
    per_peer = outs[0].shape[2]
    total = pos.shape[1]
    lane = lax.broadcasted_iota(jnp.int32, (1, per_peer), 1)
    me = lax.axis_index("width")
    for copy in copies:
        copy.wait()
    for n, out in enumerate(outs):
        for side in range(2):
            r = me ^ (2 * n + side)
            part = pl.ds(pl.multiple_of(r * per_peer, SLOT), per_peer)
            out[side, 0:3] = pos[:, part]
            out[side, 3:6] = vor[:, part]
            out[side, 6:7] = jnp.where(lane < counts[0, r], ids[:, part], total).astype(f32)
            out[side, 7:8] = jnp.zeros((1, per_peer), f32)


def add_records(records, acc, fresh):
    per_peer = records.shape[1]
    highs = acc.shape[0] // 16
    row = lax.broadcasted_iota(jnp.int32, (8, per_peer), 0)
    low_index = lax.broadcasted_iota(jnp.int32, (LOW, per_peer), 0).astype(f32).astype(bf16)
    ids = records[6:7]
    id_high = jnp.floor(ids * (1.0 / LOW))
    id_low = ids - id_high * LOW
    kept = jnp.where(row == 6, 1.0, records)
    high, low = split2(kept)
    pieces = jnp.concatenate([high, low], axis=0).astype(bf16)
    high_b = jnp.broadcast_to(id_high, (16, per_peer)).astype(bf16)
    zero = jnp.zeros_like(pieces)
    lhs = jnp.concatenate(
        [jnp.where(high_b == jnp.asarray(h, bf16), pieces, zero) for h in range(highs)], axis=0
    )
    low_b = jnp.broadcast_to(id_low, (LOW, per_peer)).astype(bf16)
    rhs = jnp.where(low_b == low_index, jnp.ones((), bf16), jnp.zeros((), bf16))
    term = lax.dot_general(lhs, rhs, (((1,), (1,)), ((), ())), preferred_element_type=f32)
    if fresh:
        acc[...] = term
    else:
        acc[...] += term


def forward_kernel(*refs):
    *arrived, out = refs
    for n, chunk in enumerate(arrived):
        out[n] = chunk[1]


def scatter_near_kernel(*refs):
    *arrived, acc = refs
    for n, chunk in enumerate(arrived):
        add_records(chunk[0], acc, n == 0)


def scatter_kernel(first, arrived, boxes, row_a, row_b, left, right, acc):
    highs = acc.shape[0] // 16
    for n in range(arrived.shape[0]):
        add_records(arrived[n], acc, n == 0)
    rows_here, cols_here = boxes.shape[:2]
    for h in range(highs):
        both = acc[16 * h : 16 * h + 16] + first[16 * h : 16 * h + 16]
        block = both[:8] + both[8:]
        for k in range(LOW // SLOT):
            i, j = divmod(h * (LOW // SLOT) + k, cols_here)
            piece = block[:, k * SLOT : (k + 1) * SLOT]
            boxes[i, j] = piece
            if j == 0:
                left[i] = piece
            if j == cols_here - 1:
                right[i] = piece
    even = (lax.axis_index("flow") & 1) == 0
    row_a[...] = jnp.where(even, boxes[rows_here - 1], boxes[0])
    row_b[...] = jnp.where(even, boxes[0], boxes[rows_here - 1])


def moments_kernel(offset, tops, boxes, out, acc):
    count = boxes.shape[0] // 8
    rows_here = tops.shape[0]

    def line(block):
        return jnp.concatenate([block[i : i + 1] for i in range(rows_here)] * 2, axis=1)

    fields = []
    for f in range(6):
        plane = boxes[pl.ds(f, count, stride=8), :]
        both = jnp.concatenate([plane, pltpu.roll(plane, SLOT - count, 1)], axis=0)
        field = jnp.transpose(both)[:count]
        fields.append(field + line(offset[f]) if f < 3 else field)
    index = {t: m for m, t in enumerate(TERMS)}
    chunk = MOMENT_ROWS
    for k in range(count // chunk):
        part = slice(k * chunk, (k + 1) * chunk)
        powers = []
        for f in range(3):
            x = fields[f][part]
            column = [None, x]
            for d in range(2, ORDER + 1):
                column.append(column[-1] * (x * (1.0 / d)))
            powers.append(column)
        spins = [fields[3 + f][part] for f in range(3)]
        for c in range(3):
            for a in range(ORDER + 1):
                lead_a = spins[c] if a == 0 else spins[c] * powers[0][a]
                for b in range(ORDER + 1 - a):
                    lead = lead_a if b == 0 else lead_a * powers[1][b]
                    for n in range(ORDER + 1 - a - b):
                        value = lead if n == 0 else lead * powers[2][n]
                        while value.shape[0] > 8:
                            half = value.shape[0] // 2
                            value = value[:half] + value[half:]
                        at = c * N_TERMS + index[(a, b, n)]
                        if k == 0:
                            acc[8 * at : 8 * at + 8] = value
                        else:
                            acc[8 * at : 8 * at + 8] += value
    acc[8 * COEF : 8 * COEF + 8] = jnp.zeros((8, SLOT), f32)
    total = acc[pl.ds(0, 2 * HALF_ROWS, stride=8), :]
    for s in range(1, 8):
        total = total + acc[pl.ds(s, 2 * HALF_ROWS, stride=8), :]
    total = total + pltpu.roll(total, count, 1)
    lane = lax.broadcasted_iota(jnp.int32, (HALF_ROWS, SLOT), 1)
    out[...] = jnp.where(lane < count, total[:HALF_ROWS], total[HALF_ROWS:])
    last = out[HALF_ROWS - 1 : HALF_ROWS, :]
    ids = line(tops[...].astype(f32))
    out[HALF_ROWS - 1 : HALF_ROWS, :] = jnp.where(lane[:1] < count, last, ids)


def tops_kernel(*refs):
    *shares, out = refs
    shares = [share[n] for share in shares for n in range(share.shape[0])]
    tops_here = out.shape[2]
    base = lax.axis_index("flow") * tops_here
    lane = lax.broadcasted_iota(jnp.int32, (HALF_ROWS, SLOT), 1)
    wanted = (lax.broadcasted_iota(jnp.int32, (tops_here, SLOT), 0) + base).astype(f32)
    half = SLOT // 2
    total = None
    for f in range(0, len(shares), 2):
        one, two = shares[f], shares[f + 1]
        upper = jnp.where(lane < half, one, pltpu.roll(two, half, 1))
        lower = jnp.where(lane < half, pltpu.roll(one, half, 1), two)
        member = jnp.where(wanted == lower[HALF_ROWS - 1 : HALF_ROWS], 1.0, 0.0).astype(bf16)
        rest = jnp.concatenate([upper, lower], axis=0)
        for _ in range(3):
            piece = rest.astype(bf16)
            rest = rest - piece.astype(f32)
            term = lax.dot_general(
                piece, member, (((1,), (1,)), ((), ())), preferred_element_type=f32
            )
            total = term if total is None else total + term
    out[:, 0, :] = total[:COEF]


def near_kernel(
    pairs, center, row_a, row_b, col_a, col_b, out, pad, feat, target, raw, weight, shifts, masks, k_high, k_low, sums
):
    rows_here, cols_here = center.shape[:2]
    count = rows_here * cols_here
    wide = cols_here + 2
    boxes_all = (rows_here + 2) * wide
    row = rows8()

    def at8(b):
        return pl.ds(b * 8 if isinstance(b, int) else pl.multiple_of(b * 8, 8), 8)

    def field_of(ref, first, f):
        return ref[pl.ds(first * 8 + f, 8, stride=8), :]

    even_f = (lax.axis_index("flow") & 1) == 0
    even_w = (lax.axis_index("width") & 1) == 0
    for j in range(cols_here):
        for i in range(rows_here):
            pad[at8((i + 1) * wide + 1 + j), :] = center[i, j]
        pad[at8(1 + j), :] = jnp.where(even_f, row_b[j], row_a[j])
        pad[at8((rows_here + 1) * wide + 1 + j), :] = jnp.where(even_f, row_a[j], row_b[j])
    for i in range(rows_here + 2):
        pad[at8(i * wide), :] = jnp.where(even_w, col_b[i], col_a[i])
        pad[at8(i * wide + wide - 1), :] = jnp.where(even_w, col_a[i], col_b[i])
    zeros8 = jnp.zeros((8, SLOT), f32)
    for b in range(boxes_all, pad.shape[0] // 8):
        pad[at8(b), :] = zeros8

    for k in range(9):
        d0, d1 = float(k // 3 - 1), float(k % 3 - 1)
        a_rows = [-d0, -d1, 0.0, -d0, -d1, 0.0, d0 * d0 + d1 * d1, 0.0]
        b_rows = [-2 * d0, -2 * d1, 0.0, -2 * d0, -2 * d1, 0.0, 1.0, 1.0]
        tile_a, tile_b = zeros8, zeros8
        for r in range(8):
            tile_a = jnp.where(row == r, a_rows[r], tile_a)
            tile_b = jnp.where(row == r, b_rows[r], tile_b)
        shifts[k] = jnp.concatenate([tile_a, tile_b], axis=0).astype(bf16)
        turns = jnp.zeros((8, SLOT), f32)
        for r, value in enumerate((d1, d0, d0, d1)):
            turns = jnp.where(row == r, value, turns)
        masks[k] = jnp.concatenate([zeros8 + 1.0, turns] * 2, axis=0).astype(bf16)

    for start in range(0, boxes_all, 8):
        y0, y1, y2, w0, w1, w2 = (field_of(pad, start, f) for f in range(6))
        values = [w0, w1, w2, y1 * w2 - y2 * w1, y2 * w0 - y0 * w2, y0 * w1 - y1 * w0, zeros8, zeros8]
        values += [w2, w2, w1, w0] + [zeros8] * 4
        for f, value in enumerate(values):
            raw[pl.ds(start * 16 + f, 8, stride=16), :] = value
        pad[pl.ds(start * 8 + 7, 8, stride=8), :] = y0 * y0 + y1 * y1 + y2 * y2

    def prepare(at, _):
        y = pad[at8(at), :]
        norm = jnp.broadcast_to(y[7:8], (8, SLOT))
        high, low = split2(y)
        turned = pltpu.roll(low, 3, 0)
        n1, rest = split2(norm)
        n2, rest = split2(rest)
        first = jnp.where(row < 3, -2.0 * high, jnp.where(row < 6, -2.0 * turned, 1.0))
        second = jnp.where(row == 7, n1, first)
        fourth = jnp.where(row == 6, n2, jnp.where(row == 7, rest, 1.0))
        feat[at, 0:16] = jnp.concatenate([first, second], axis=0).astype(bf16)
        feat[at, 16:32] = jnp.concatenate([first, fourth], axis=0).astype(bf16)
        high, low = split2(raw[pl.ds(pl.multiple_of(at * 16, 16), 16), :])
        weight[at] = jnp.concatenate([high, low], axis=0).astype(bf16)
        return 0

    lax.fori_loop(0, boxes_all, prepare, 0, unroll=6)

    const_row = jnp.where((row == 2) | (row == 5) | (row == 7), 0.0, 1.0)

    def place(b):
        i = lax.div(b, cols_here) if cols_here & (cols_here - 1) else b >> (cols_here.bit_length() - 1)
        return i, b - i * cols_here

    def sources(b):
        i, j = place(b)
        corner = i * wide + j
        found = [(4, None, None, corner + wide + 1)]
        for q in range(pairs.shape[0]):
            code = pairs[q, i, j]
            k = jnp.where(code >= 4, code + 1, code)
            r = (k * 11) >> 5
            c = k - 3 * r
            found.append((k, r, c, corner + r * wide + c))
        return found

    def target_stage(b, slot):
        i, j = place(b)
        x = pad[at8((i + 1) * wide + 1 + j), :]
        high, low = split2(x)
        a1, rest = split2(jnp.broadcast_to(x[7:8], (8, SLOT)) + core_sq)
        a2, a3 = split2(rest)
        high3, low3 = pltpu.roll(high, 3, 0), pltpu.roll(low, 3, 0)
        rows = [
            jnp.where(row < 3, high, jnp.where(row < 6, high3, jnp.where(row == 6, a1, a2))),
            jnp.where(row < 3, low, jnp.where(row < 6, low3, jnp.where(row == 6, a3, 1.0))),
            const_row,
            jnp.where(row < 3, high, jnp.where(row < 6, low3, 1.0)),
        ]
        target[slot] = jnp.transpose(jnp.concatenate(rows, axis=0).astype(bf16))

    def kernel_stage(b, slot):
        features = []
        for k, _, _, source in sources(b):
            second = feat[source, 16:32] * shifts[k]
            features.append(jnp.concatenate([feat[source, 0:16], second], axis=0))
        feature = jnp.concatenate(features, axis=1)
        dist = lax.dot_general(
            target[slot], feature, (((1,), (0,)), ((), ())), preferred_element_type=f32
        )
        root = lax.rsqrt(dist)
        kernel = root * root * root
        high = kernel.astype(bf16)
        k_high[slot] = high
        k_low[slot] = (kernel - high.astype(f32)).astype(bf16)

    def field_stage(b, slot):
        tiles = [weight[source] * masks[k] for k, _, _, source in sources(b)]
        lhs = jnp.concatenate(tiles, axis=1)
        dims = (((1,), (1,)), ((), ()))
        main = lax.dot_general(lhs, k_high[slot], dims, preferred_element_type=f32)
        rest = lax.dot_general(lhs[0:16], k_low[slot], dims, preferred_element_type=f32)
        sums[0, at8(b), :] = main[0:8] + main[16:24] + rest[0:8]
        sums[1, at8(b), :] = main[8:16] + main[24:32] + rest[8:16]

    slots = k_high.shape[0]
    for u in range(LAG + 1):
        target_stage(u, u)
    for u in range(LAG):
        kernel_stage(u, u)

    def some_boxes(t, _):
        for u in range(slots):
            b = slots * t + u
            kernel_stage(jnp.minimum(b + LAG, count - 1), (u + LAG) % slots)
            field_stage(b, u)
            target_stage(jnp.minimum(b + LAG + 1, count - 1), (u + LAG + 1) % slots)
        return 0

    lax.fori_loop(0, count // slots, some_boxes, 0)

    for i in range(rows_here):
        for j in range(0, cols_here, 8):
            at = (i + 1) * wide + 1 + j
            b = i * cols_here + j
            x0, x1, x2 = (field_of(pad, at, f) for f in range(3))
            scale = -inv_four_pi * field_of(pad, at, 6)
            a0, a1, a2, b0, b1, b2 = (field_of(sums.at[0], b, f) for f in range(6))
            h0, h1, h2, h3 = (field_of(sums.at[1], b, f) for f in range(4))
            out[0, i, j : j + 8, :] = scale * (x1 * a2 - x2 * a1 - (b0 + h0))
            out[1, i, j : j + 8, :] = scale * (x2 * a0 - x0 * a2 - (b1 - h1))
            out[2, i, j : j + 8, :] = scale * (x0 * a1 - x1 * a0 - (b2 + h2 - h3))


def spec(space):
    return pl.BlockSpec(memory_space=space)


def call(kernel, out_shape, spaces, scratch=(), cost=(0, 0), name=None, limit=8):
    many = isinstance(out_shape, (list, tuple))
    return pl.pallas_call(
        kernel,
        out_shape=out_shape,
        in_specs=[spec(s) for s in spaces],
        out_specs=[spec(VMEM)] * len(out_shape) if many else spec(VMEM),
        scratch_shapes=list(scratch),
        compiler_params=pltpu.CompilerParams(vmem_limit_bytes=limit * 1024 * 1024),
        cost_estimate=pl.CostEstimate(flops=cost[0], bytes_accessed=cost[1], transcendentals=0),
        name=name,
    )


def shape(*dims):
    return jax.ShapeDtypeStruct(dims, f32)


def in_hbm(x):
    return pltpu.with_memory_space_constraint(x, pltpu.HBM)


def swap(axis, step):
    return [(i, i ^ step) for i in range(lax.axis_size(axis))]


def swap_odd(axis):
    odd = range(1, lax.axis_size(axis) - 1, 2)
    return [(i, i + 1) for i in odd] + [(i + 1, i) for i in odd]


def shards(positions, vorticity, dest_slot, send_counts, near_pairs, box_top, box_offset):
    slot_total = positions.shape[1]
    peers = lax.axis_size("width")
    flows = lax.axis_size("flow")
    per_peer = slot_total // peers
    rows_here, cols_here = box_top.shape
    count = rows_here * cols_here
    outgoing = call(
        pack_kernel,
        [shape(2, 8, per_peer)] * (peers // 2),
        [SMEM, pltpu.HBM, pltpu.HBM, pltpu.HBM],
        [
            VMEM((3, slot_total), f32),
            VMEM((3, slot_total), f32),
            VMEM((1, slot_total), jnp.int32),
            pltpu.SemaphoreType.DMA((3,)),
        ],
        name="pack",
    )(
        in_hbm(send_counts),
        in_hbm(positions),
        in_hbm(vorticity),
        in_hbm(dest_slot.reshape(1, slot_total)),
    )
    arrived = [
        lax.ppermute(outgoing[n], "width", swap("width", 2 * n))
        for n in range(peers // 2 - 1, 0, -1)
    ]
    arrived.append(outgoing[0])
    passed = call(
        forward_kernel, shape(len(arrived), 8, per_peer), [VMEM] * len(arrived), name="forward"
    )(*arrived)
    passed = lax.ppermute(passed, "width", swap("width", 1))
    part = call(
        scatter_near_kernel,
        shape(slot_total // LOW * 16, LOW),
        [VMEM] * len(arrived),
        cost=(5_000_000_000, 1_000_000),
        name="scatter_near",
    )(*arrived)
    boxes, row_a, row_b, left, right = call(
        scatter_kernel,
        [shape(rows_here, cols_here, 8, SLOT)]
        + [shape(cols_here, 8, SLOT)] * 2
        + [shape(rows_here, 8, SLOT)] * 2,
        [VMEM] * 2,
        [VMEM((slot_total // LOW * 16, LOW), f32)],
        name="scatter",
    )(part, passed)
    row_b = lax.ppermute(row_b, "flow", swap_odd("flow"))
    row_a = lax.ppermute(row_a, "flow", swap("flow", 1))
    local = call(
        moments_kernel,
        shape(HALF_ROWS, SLOT),
        [VMEM, VMEM, VMEM],
        [VMEM((16 * HALF_ROWS + 8, SLOT), f32)],
        cost=(10_000_000, 1_000_000),
        name="moments",
    )(in_hbm(box_offset), in_hbm(box_top), boxes.reshape(8 * count, SLOT))
    shares = [local[None]]
    for s in range(1, flows):
        shares.append(lax.ppermute(local, "flow", swap("flow", s))[None])
    even_f = (lax.axis_index("flow") & 1) == 0
    even_w = (lax.axis_index("width") & 1) == 0
    up = jnp.where(even_f, row_b, row_a)
    down = jnp.where(even_f, row_a, row_b)
    left = jnp.concatenate([up[:1], left, down[:1]], axis=0)
    right = jnp.concatenate([up[cols_here - 1 :], right, down[cols_here - 1 :]], axis=0)
    left, right, _ = lax.optimization_barrier((left, right, local))
    col_b = lax.ppermute(jnp.where(even_w, left, right), "width", swap_odd("width"))
    col_a = lax.ppermute(jnp.where(even_w, right, left), "width", swap("width", 1))
    padded = -(-(rows_here + 2) * (cols_here + 2) // 8) * 8
    velocity = call(
        near_kernel,
        shape(3, rows_here, cols_here, SLOT),
        [SMEM] + [VMEM] * 5,
        [
            VMEM((8 * padded, SLOT), f32),
            VMEM((padded, 32, SLOT), bf16),
            VMEM((UNROLL, SLOT, 32), bf16),
            VMEM((16 * padded, SLOT), f32),
            VMEM((padded, 32, SLOT), bf16),
            VMEM((9, 16, SLOT), bf16),
            VMEM((9, 32, SLOT), bf16),
            VMEM((UNROLL, SLOT, 4 * SLOT), bf16),
            VMEM((UNROLL, SLOT, 4 * SLOT), bf16),
            VMEM((2, 8 * count, SLOT), f32),
        ],
        cost=(5_000_000_000, 2_000_000),
        name="near",
        limit=28,
    )(in_hbm(near_pairs.transpose(2, 0, 1)), boxes, row_a, row_b, col_a, col_b)
    tops_here = TOP // flows
    summed = call(tops_kernel, shape(COEF, 1, tops_here), [VMEM] * len(shares), name="tops")(
        *shares
    )
    return (velocity, summed.transpose(1, 2, 0))


def solution(mesh):
    placed = (
        P(None, ("flow", "width")),
        P(None, ("flow", "width")),
        P(("flow", "width")),
        P(("flow", "width"), None),
        P("flow", "width", None),
        P("flow", "width"),
        P(None, "flow", "width"),
    )
    return jax.shard_map(
        shards,
        mesh=mesh,
        in_specs=placed,
        out_specs=(P(None, "flow", "width", None), P("width", "flow", None)),
        check_vma=False,
    )
```

```python
import functools
import math

import jax
import jax.numpy as jnp
from jax import lax
from jax.experimental import pallas as pl
from jax.experimental.pallas import tpu as pltpu
from jax.sharding import PartitionSpec as P

SLOT = 128
ORDER = 8
TOP = 1024
TERMS = [
    (a, b, s - a - b)
    for s in range(ORDER + 1)
    for a in range(s, -1, -1)
    for b in range(s - a, -1, -1)
]
N_TERMS = len(TERMS)
COEF = 3 * N_TERMS
HALF_ROWS = (COEF + 1) // 2
LAG = 2
MOMENT_ROWS = 16
UNROLL = 32
LOW = 256

core_sq = 0.25
inv_four_pi = 0.07957747154594767
f32 = jnp.float32
bf16 = jnp.bfloat16
VMEM = pltpu.VMEM
SMEM = pltpu.SMEM


def split2(x):
    high = x.astype(bf16).astype(f32)
    return high, x - high


def rows8(x_shape=(8, SLOT)):
    return lax.broadcasted_iota(jnp.int32, x_shape, 0)


def pack_kernel(send_counts, positions, vorticity, dest, *refs):
    *outs, pos, vor, ids, counts, sems = refs
    copies = [
        pltpu.make_async_copy(src, dst, sems.at[n])
        for n, (src, dst) in enumerate(
            [(positions, pos), (vorticity, vor), (dest, ids), (send_counts, counts)]
        )
    ]
    for copy in copies:
        copy.start()
    per_peer = outs[0].shape[2]
    total = pos.shape[1]
    lane = lax.broadcasted_iota(jnp.int32, (1, per_peer), 1)
    me = lax.axis_index("width")
    for copy in copies:
        copy.wait()
    for n, out in enumerate(outs):
        for side in range(2):
            r = me ^ (2 * n + side)
            part = pl.ds(pl.multiple_of(r * per_peer, SLOT), per_peer)
            out[side, 0:3] = pos[:, part]
            out[side, 3:6] = vor[:, part]
            out[side, 6:7] = jnp.where(lane < counts[0, r], ids[:, part], total).astype(f32)
            out[side, 7:8] = jnp.zeros((1, per_peer), f32)


def add_records(records, acc, fresh):
    per_peer = records.shape[1]
    highs = acc.shape[0] // 16
    row = lax.broadcasted_iota(jnp.int32, (8, per_peer), 0)
    low_index = lax.broadcasted_iota(jnp.int32, (LOW, per_peer), 0).astype(f32).astype(bf16)
    ids = records[6:7]
    id_high = jnp.floor(ids * (1.0 / LOW))
    id_low = ids - id_high * LOW
    kept = jnp.where(row == 6, 1.0, records)
    high, low = split2(kept)
    pieces = jnp.concatenate([high, low], axis=0).astype(bf16)
    high_b = jnp.broadcast_to(id_high, (16, per_peer)).astype(bf16)
    zero = jnp.zeros_like(pieces)
    lhs = jnp.concatenate(
        [jnp.where(high_b == jnp.asarray(h, bf16), pieces, zero) for h in range(highs)], axis=0
    )
    low_b = jnp.broadcast_to(id_low, (LOW, per_peer)).astype(bf16)
    rhs = jnp.where(low_b == low_index, jnp.ones((), bf16), jnp.zeros((), bf16))
    term = lax.dot_general(lhs, rhs, (((1,), (1,)), ((), ())), preferred_element_type=f32)
    if fresh:
        acc[...] = term
    else:
        acc[...] += term


def forward_kernel(*refs):
    *arrived, out = refs
    for n, chunk in enumerate(arrived):
        out[n] = chunk[1]


def scatter_near_kernel(*refs):
    *arrived, acc = refs
    for n, chunk in enumerate(arrived):
        add_records(chunk[0], acc, n == 0)


def scatter_kernel(first, arrived, boxes, row_a, row_b, left, right, acc):
    highs = acc.shape[0] // 16
    for n in range(arrived.shape[0]):
        add_records(arrived[n], acc, n == 0)
    rows_here, cols_here = boxes.shape[:2]
    for h in range(highs):
        both = acc[16 * h : 16 * h + 16] + first[16 * h : 16 * h + 16]
        block = both[:8] + both[8:]
        for k in range(LOW // SLOT):
            i, j = divmod(h * (LOW // SLOT) + k, cols_here)
            piece = block[:, k * SLOT : (k + 1) * SLOT]
            boxes[i, j] = piece
            if j == 0:
                left[i] = piece
            if j == cols_here - 1:
                right[i] = piece
    even = (lax.axis_index("flow") & 1) == 0
    row_a[...] = jnp.where(even, boxes[rows_here - 1], boxes[0])
    row_b[...] = jnp.where(even, boxes[0], boxes[rows_here - 1])


def edges_kernel(row_a, row_b, left, right, col_a, col_b):
    even_f = (lax.axis_index("flow") & 1) == 0
    even_w = (lax.axis_index("width") & 1) == 0
    rows_here, last = left.shape[0], row_a.shape[0] - 1

    def column(edge, at):
        one, two = row_a[at], row_b[at]
        return [jnp.where(even_f, two, one)] + [edge[i] for i in range(rows_here)] + [
            jnp.where(even_f, one, two)
        ]

    for i, (low, high) in enumerate(zip(column(left, 0), column(right, last))):
        col_a[i] = jnp.where(even_w, high, low)
        col_b[i] = jnp.where(even_w, low, high)


def moments_kernel(offset_hbm, tops_hbm, boxes, out, acc, offset, tops, sems):
    copies = [
        pltpu.make_async_copy(offset_hbm, offset, sems.at[0]),
        pltpu.make_async_copy(tops_hbm, tops, sems.at[1]),
    ]
    for copy in copies:
        copy.start()
    count = boxes.shape[0] // 8
    rows_here = tops.shape[0]

    def line(block):
        return jnp.concatenate([block[i : i + 1] for i in range(rows_here)] * 2, axis=1)

    fields = []
    for f in range(6):
        plane = boxes[pl.ds(f, count, stride=8), :]
        both = jnp.concatenate([plane, pltpu.roll(plane, SLOT - count, 1)], axis=0)
        fields.append(jnp.transpose(both)[:count])
    for copy in copies:
        copy.wait()
    fields = [x + line(offset[f]) if f < 3 else x for f, x in enumerate(fields)]
    index = {t: m for m, t in enumerate(TERMS)}
    chunk = MOMENT_ROWS
    for k in range(count // chunk):
        part = slice(k * chunk, (k + 1) * chunk)
        powers = []
        for f in range(3):
            x = fields[f][part]
            column = [None, x]
            for d in range(2, ORDER + 1):
                column.append(column[-1] * (x * (1.0 / d)))
            powers.append(column)
        spins = [fields[3 + f][part] for f in range(3)]
        for c in range(3):
            for a in range(ORDER + 1):
                lead_a = spins[c] if a == 0 else spins[c] * powers[0][a]
                for b in range(ORDER + 1 - a):
                    lead = lead_a if b == 0 else lead_a * powers[1][b]
                    for n in range(ORDER + 1 - a - b):
                        value = lead if n == 0 else lead * powers[2][n]
                        while value.shape[0] > 8:
                            half = value.shape[0] // 2
                            value = value[:half] + value[half:]
                        at = c * N_TERMS + index[(a, b, n)]
                        if k == 0:
                            acc[8 * at : 8 * at + 8] = value
                        else:
                            acc[8 * at : 8 * at + 8] += value
    acc[8 * COEF : 8 * COEF + 8] = jnp.zeros((8, SLOT), f32)
    total = acc[pl.ds(0, 2 * HALF_ROWS, stride=8), :]
    for s in range(1, 8):
        total = total + acc[pl.ds(s, 2 * HALF_ROWS, stride=8), :]
    total = total + pltpu.roll(total, count, 1)
    lane = lax.broadcasted_iota(jnp.int32, (HALF_ROWS, SLOT), 1)
    out[...] = jnp.where(lane < count, total[:HALF_ROWS], total[HALF_ROWS:])
    last = out[HALF_ROWS - 1 : HALF_ROWS, :]
    ids = line(tops[...].astype(f32))
    out[HALF_ROWS - 1 : HALF_ROWS, :] = jnp.where(lane[:1] < count, last, ids)


def tops_kernel(*refs):
    *shares, out, ready, sems = refs
    shares = [share[n] for share in shares for n in range(share.shape[0])]
    tops_here = out.shape[2]
    base = lax.axis_index("flow") * tops_here
    lane = lax.broadcasted_iota(jnp.int32, (HALF_ROWS, SLOT), 1)
    wanted = (lax.broadcasted_iota(jnp.int32, (tops_here, SLOT), 0) + base).astype(f32)
    half = SLOT // 2
    pairs = [(shares[f], shares[f + 1]) for f in range(0, len(shares), 2)]
    last = slice(HALF_ROWS - 1, HALF_ROWS)
    members = []
    for one, two in pairs:
        ids = jnp.where(lane[:1] < half, pltpu.roll(one[last], half, 1), two[last])
        members.append(jnp.where(wanted == ids, 1.0, 0.0).astype(bf16))
    copies = []
    for n in range(2):
        total = None
        for (one, two), member in zip(pairs, members):
            if n == 0:
                rest = jnp.where(lane < half, one, pltpu.roll(two, half, 1))
            else:
                rest = jnp.where(lane < half, pltpu.roll(one, half, 1), two)
            for _ in range(3):
                piece = rest.astype(bf16)
                rest = rest - piece.astype(f32)
                term = lax.dot_general(
                    piece, member, (((1,), (1,)), ((), ())), preferred_element_type=f32
                )
                total = term if total is None else total + term
        rows = min(HALF_ROWS, COEF - n * HALF_ROWS)
        part = pl.ds(n * HALF_ROWS, rows)
        ready[part, 0, :] = total[:rows]
        copies.append(pltpu.make_async_copy(ready.at[part], out.at[part], sems.at[n]))
        copies[-1].start()
    for copy in copies:
        copy.wait()


def near_kernel(
    codes, center, row_a, row_b, col_a, col_b, out, pad, feat, target, raw, weight, shifts, masks, k_high, k_low, sums, pairs, sem
):
    rows_here, cols_here = center.shape[:2]
    count = rows_here * cols_here
    wide = cols_here + 2
    boxes_all = (rows_here + 2) * wide
    row = rows8()

    listed = pltpu.make_async_copy(codes, pairs, sem)
    listed.start()

    def at8(b):
        return pl.ds(b * 8 if isinstance(b, int) else pl.multiple_of(b * 8, 8), 8)

    def field_of(ref, first, f):
        return ref[pl.ds(first * 8 + f, 8, stride=8), :]

    even_f = (lax.axis_index("flow") & 1) == 0
    even_w = (lax.axis_index("width") & 1) == 0
    for j in range(cols_here):
        for i in range(rows_here):
            pad[at8((i + 1) * wide + 1 + j), :] = center[i, j]
        pad[at8(1 + j), :] = jnp.where(even_f, row_b[j], row_a[j])
        pad[at8((rows_here + 1) * wide + 1 + j), :] = jnp.where(even_f, row_a[j], row_b[j])
    for i in range(rows_here + 2):
        pad[at8(i * wide), :] = jnp.where(even_w, col_b[i], col_a[i])
        pad[at8(i * wide + wide - 1), :] = jnp.where(even_w, col_a[i], col_b[i])
    zeros8 = jnp.zeros((8, SLOT), f32)
    for b in range(boxes_all, pad.shape[0] // 8):
        pad[at8(b), :] = zeros8

    for k in range(9):
        d0, d1 = float(k // 3 - 1), float(k % 3 - 1)
        a_rows = [-d0, -d1, 0.0, -d0, -d1, 0.0, d0 * d0 + d1 * d1, 0.0]
        b_rows = [-2 * d0, -2 * d1, 0.0, -2 * d0, -2 * d1, 0.0, 1.0, 1.0]
        tile_a, tile_b = zeros8, zeros8
        for r in range(8):
            tile_a = jnp.where(row == r, a_rows[r], tile_a)
            tile_b = jnp.where(row == r, b_rows[r], tile_b)
        shifts[k] = jnp.concatenate([tile_a, tile_b], axis=0).astype(bf16)
        turns = jnp.zeros((8, SLOT), f32)
        for r, value in enumerate((d1, d0, d0, d1)):
            turns = jnp.where(row == r, value, turns)
        masks[k] = jnp.concatenate([zeros8 + 1.0, turns] * 2, axis=0).astype(bf16)

    for start in range(0, boxes_all, 8):
        y0, y1, y2, w0, w1, w2 = (field_of(pad, start, f) for f in range(6))
        values = [w0, w1, w2, y1 * w2 - y2 * w1, y2 * w0 - y0 * w2, y0 * w1 - y1 * w0, zeros8, zeros8]
        values += [w2, w2, w1, w0] + [zeros8] * 4
        for f, value in enumerate(values):
            raw[pl.ds(start * 16 + f, 8, stride=16), :] = value
        pad[pl.ds(start * 8 + 7, 8, stride=8), :] = y0 * y0 + y1 * y1 + y2 * y2

    def prepare(at, _):
        y = pad[at8(at), :]
        norm = jnp.broadcast_to(y[7:8], (8, SLOT))
        high, low = split2(y)
        turned = pltpu.roll(low, 3, 0)
        n1, rest = split2(norm)
        n2, rest = split2(rest)
        first = jnp.where(row < 3, -2.0 * high, jnp.where(row < 6, -2.0 * turned, 1.0))
        second = jnp.where(row == 7, n1, first)
        fourth = jnp.where(row == 6, n2, jnp.where(row == 7, rest, 1.0))
        feat[at, 0:16] = jnp.concatenate([first, second], axis=0).astype(bf16)
        feat[at, 16:32] = jnp.concatenate([first, fourth], axis=0).astype(bf16)
        high, low = split2(raw[pl.ds(pl.multiple_of(at * 16, 16), 16), :])
        weight[at] = jnp.concatenate([high, low], axis=0).astype(bf16)
        return 0

    lax.fori_loop(0, boxes_all, prepare, 0, unroll=6)

    const_row = jnp.where((row == 2) | (row == 5) | (row == 7), 0.0, 1.0)

    def place(b):
        i = lax.div(b, cols_here) if cols_here & (cols_here - 1) else b >> (cols_here.bit_length() - 1)
        return i, b - i * cols_here

    def sources(b):
        i, j = place(b)
        corner = i * wide + j
        found = [(4, None, None, corner + wide + 1)]
        for q in range(pairs.shape[0]):
            code = pairs[q, i, j]
            k = jnp.where(code >= 4, code + 1, code)
            r = (k * 11) >> 5
            c = k - 3 * r
            found.append((k, r, c, corner + r * wide + c))
        return found

    def target_stage(b, slot):
        i, j = place(b)
        x = pad[at8((i + 1) * wide + 1 + j), :]
        high, low = split2(x)
        a1, rest = split2(jnp.broadcast_to(x[7:8], (8, SLOT)) + core_sq)
        a2, a3 = split2(rest)
        high3, low3 = pltpu.roll(high, 3, 0), pltpu.roll(low, 3, 0)
        rows = [
            jnp.where(row < 3, high, jnp.where(row < 6, high3, jnp.where(row == 6, a1, a2))),
            jnp.where(row < 3, low, jnp.where(row < 6, low3, jnp.where(row == 6, a3, 1.0))),
            const_row,
            jnp.where(row < 3, high, jnp.where(row < 6, low3, 1.0)),
        ]
        target[slot] = jnp.transpose(jnp.concatenate(rows, axis=0).astype(bf16))

    def kernel_stage(b, slot):
        features = []
        for k, _, _, source in sources(b):
            second = feat[source, 16:32] * shifts[k]
            features.append(jnp.concatenate([feat[source, 0:16], second], axis=0))
        feature = jnp.concatenate(features, axis=1)
        dist = lax.dot_general(
            target[slot], feature, (((1,), (0,)), ((), ())), preferred_element_type=f32
        )
        root = lax.rsqrt(dist)
        kernel = root * root * root
        high = kernel.astype(bf16)
        k_high[slot] = high
        k_low[slot] = (kernel - high.astype(f32)).astype(bf16)

    def field_stage(b, slot):
        tiles = [weight[source] * masks[k] for k, _, _, source in sources(b)]
        lhs = jnp.concatenate(tiles, axis=1)
        dims = (((1,), (1,)), ((), ()))
        main = lax.dot_general(lhs, k_high[slot], dims, preferred_element_type=f32)
        rest = lax.dot_general(lhs[0:16], k_low[slot], dims, preferred_element_type=f32)
        sums[0, at8(b), :] = main[0:8] + main[16:24] + rest[0:8]
        sums[1, at8(b), :] = main[8:16] + main[24:32] + rest[8:16]

    listed.wait()
    slots = k_high.shape[0]
    for u in range(LAG + 1):
        target_stage(u, u)
    for u in range(LAG):
        kernel_stage(u, u)

    def some_boxes(t, _):
        for u in range(slots):
            b = slots * t + u
            kernel_stage(jnp.minimum(b + LAG, count - 1), (u + LAG) % slots)
            field_stage(b, u)
            target_stage(jnp.minimum(b + LAG + 1, count - 1), (u + LAG + 1) % slots)
        return 0

    lax.fori_loop(0, count // slots, some_boxes, 0)

    for i in range(rows_here):
        for j in range(0, cols_here, 8):
            at = (i + 1) * wide + 1 + j
            b = i * cols_here + j
            x0, x1, x2 = (field_of(pad, at, f) for f in range(3))
            scale = -inv_four_pi * field_of(pad, at, 6)
            a0, a1, a2, b0, b1, b2 = (field_of(sums.at[0], b, f) for f in range(6))
            h0, h1, h2, h3 = (field_of(sums.at[1], b, f) for f in range(4))
            out[0, i, j : j + 8, :] = scale * (x1 * a2 - x2 * a1 - (b0 + h0))
            out[1, i, j : j + 8, :] = scale * (x2 * a0 - x0 * a2 - (b1 - h1))
            out[2, i, j : j + 8, :] = scale * (x0 * a1 - x1 * a0 - (b2 + h2 - h3))


def spec(space):
    return pl.BlockSpec(memory_space=space)


def call(kernel, out_shape, spaces, scratch=(), cost=(0, 0), name=None, limit=8, out_space=VMEM):
    many = isinstance(out_shape, (list, tuple))
    return pl.pallas_call(
        kernel,
        out_shape=out_shape,
        in_specs=[spec(s) for s in spaces],
        out_specs=[spec(out_space)] * len(out_shape) if many else spec(out_space),
        scratch_shapes=list(scratch),
        compiler_params=pltpu.CompilerParams(vmem_limit_bytes=limit * 1024 * 1024),
        cost_estimate=pl.CostEstimate(flops=cost[0], bytes_accessed=cost[1], transcendentals=0),
        name=name,
    )


def shape(*dims):
    return jax.ShapeDtypeStruct(dims, f32)


def in_hbm(x):
    return pltpu.with_memory_space_constraint(x, pltpu.HBM)


def swap(axis, step):
    return [(i, i ^ step) for i in range(lax.axis_size(axis))]


def swap_odd(axis):
    odd = range(1, lax.axis_size(axis) - 1, 2)
    return [(i, i + 1) for i in odd] + [(i + 1, i) for i in odd]


def shards(positions, vorticity, dest_slot, send_counts, near_pairs, box_top, box_offset):
    slot_total = positions.shape[1]
    peers = lax.axis_size("width")
    flows = lax.axis_size("flow")
    per_peer = slot_total // peers
    rows_here, cols_here = box_top.shape
    count = rows_here * cols_here
    outgoing = call(
        pack_kernel,
        [shape(2, 8, per_peer)] * (peers // 2),
        [pltpu.HBM] * 4,
        [
            VMEM((3, slot_total), f32),
            VMEM((3, slot_total), f32),
            VMEM((1, slot_total), jnp.int32),
            SMEM((1, peers), jnp.int32),
            pltpu.SemaphoreType.DMA((4,)),
        ],
        name="pack",
    )(
        in_hbm(send_counts),
        in_hbm(positions),
        in_hbm(vorticity),
        in_hbm(dest_slot.reshape(1, slot_total)),
    )
    arrived = [
        lax.ppermute(outgoing[n], "width", swap("width", 2 * n))
        for n in range(peers // 2 - 1, 0, -1)
    ]
    arrived.append(outgoing[0])
    passed = call(
        forward_kernel, shape(len(arrived), 8, per_peer), [VMEM] * len(arrived), name="forward"
    )(*arrived)
    passed = lax.ppermute(passed, "width", swap("width", 1))
    part = call(
        scatter_near_kernel,
        shape(slot_total // LOW * 16, LOW),
        [VMEM] * len(arrived),
        cost=(5_000_000_000, 1_000_000),
        name="scatter_near",
    )(*arrived)
    boxes, row_a, row_b, left, right = call(
        scatter_kernel,
        [shape(rows_here, cols_here, 8, SLOT)]
        + [shape(cols_here, 8, SLOT)] * 2
        + [shape(rows_here, 8, SLOT)] * 2,
        [VMEM] * 2,
        [VMEM((slot_total // LOW * 16, LOW), f32)],
        name="scatter",
    )(part, passed)
    row_b = lax.ppermute(row_b, "flow", swap_odd("flow"))
    row_a = lax.ppermute(row_a, "flow", swap("flow", 1))
    local = call(
        moments_kernel,
        shape(HALF_ROWS, SLOT),
        [pltpu.HBM, pltpu.HBM, VMEM],
        [
            VMEM((16 * HALF_ROWS + 8, SLOT), f32),
            VMEM((3, rows_here, cols_here), f32),
            VMEM((rows_here, cols_here), jnp.int32),
            pltpu.SemaphoreType.DMA((2,)),
        ],
        cost=(10_000_000, 1_000_000),
        name="moments",
    )(in_hbm(box_offset), in_hbm(box_top), boxes.reshape(8 * count, SLOT))
    shares = [local[None]]
    for s in range(1, flows):
        shares.append(lax.ppermute(local, "flow", swap("flow", s))[None])
    row_a, row_b, _ = lax.optimization_barrier((row_a, row_b, local))
    col_a, col_b = call(
        edges_kernel, [shape(rows_here + 2, 8, SLOT)] * 2, [VMEM] * 4, name="edges"
    )(row_a, row_b, left, right)
    col_a = lax.ppermute(col_a, "width", swap("width", 1))
    col_b = lax.ppermute(col_b, "width", swap_odd("width"))
    padded = -(-(rows_here + 2) * (cols_here + 2) // 8) * 8
    velocity = call(
        near_kernel,
        shape(3, rows_here, cols_here, SLOT),
        [pltpu.HBM] + [VMEM] * 5,
        [
            VMEM((8 * padded, SLOT), f32),
            VMEM((padded, 32, SLOT), bf16),
            VMEM((UNROLL, SLOT, 32), bf16),
            VMEM((16 * padded, SLOT), f32),
            VMEM((padded, 32, SLOT), bf16),
            VMEM((9, 16, SLOT), bf16),
            VMEM((9, 32, SLOT), bf16),
            VMEM((UNROLL, SLOT, 4 * SLOT), bf16),
            VMEM((UNROLL, SLOT, 4 * SLOT), bf16),
            VMEM((2, 8 * count, SLOT), f32),
            SMEM((near_pairs.shape[2], rows_here, cols_here), jnp.int32),
            pltpu.SemaphoreType.DMA,
        ],
        cost=(5_000_000_000, 2_000_000),
        name="near",
        limit=28,
    )(in_hbm(near_pairs.transpose(2, 0, 1)), boxes, row_a, row_b, col_a, col_b)
    tops_here = TOP // flows
    summed = call(
        tops_kernel,
        shape(COEF, 1, tops_here),
        [VMEM] * len(shares),
        [VMEM((COEF, 1, tops_here), f32), pltpu.SemaphoreType.DMA((2,))],
        name="tops",
        out_space=pltpu.HBM,
    )(*shares)
    return (velocity, summed.transpose(1, 2, 0))


def solution(mesh):
    placed = (
        P(None, ("flow", "width")),
        P(None, ("flow", "width")),
        P(("flow", "width")),
        P(("flow", "width"), None),
        P("flow", "width", None),
        P("flow", "width"),
        P(None, "flow", "width"),
    )
    return jax.shard_map(
        shards,
        mesh=mesh,
        in_specs=placed,
        out_specs=(P(None, "flow", "width", None), P("width", "flow", None)),
        check_vma=False,
    )
```

```python
import functools
import math

import jax
import jax.numpy as jnp
from jax import lax
from jax.experimental import pallas as pl
from jax.experimental.pallas import tpu as pltpu
from jax.sharding import PartitionSpec as P

SLOT = 128
ORDER = 8
TOP = 1024
TERMS = [
    (a, b, s - a - b)
    for s in range(ORDER + 1)
    for a in range(s, -1, -1)
    for b in range(s - a, -1, -1)
]
N_TERMS = len(TERMS)
COEF = 3 * N_TERMS
HALF_ROWS = (COEF + 1) // 2
LAG = 2
MOMENT_ROWS = 16
UNROLL = 32
LOW = 256

core_sq = 0.25
inv_four_pi = 0.07957747154594767
f32 = jnp.float32
bf16 = jnp.bfloat16
VMEM = pltpu.VMEM
SMEM = pltpu.SMEM


def split2(x):
    high = x.astype(bf16).astype(f32)
    return high, x - high


def rows8(x_shape=(8, SLOT)):
    return lax.broadcasted_iota(jnp.int32, x_shape, 0)


def pack_kernel(send_counts, positions, vorticity, dest, *refs):
    *outs, pos, vor, ids, counts, sems = refs
    copies = [
        pltpu.make_async_copy(src, dst, sems.at[n])
        for n, (src, dst) in enumerate(
            [(positions, pos), (vorticity, vor), (dest, ids), (send_counts, counts)]
        )
    ]
    for copy in copies:
        copy.start()
    per_peer = outs[0].shape[2]
    total = pos.shape[1]
    lane = lax.broadcasted_iota(jnp.int32, (1, per_peer), 1)
    me = lax.axis_index("width")
    for copy in copies:
        copy.wait()
    for n, out in enumerate(outs):
        for side in range(2):
            r = me ^ (2 * n + side)
            part = pl.ds(pl.multiple_of(r * per_peer, SLOT), per_peer)
            out[side, 0:3] = pos[:, part]
            out[side, 3:6] = vor[:, part]
            out[side, 6:7] = jnp.where(lane < counts[0, r], ids[:, part], total).astype(f32)
            out[side, 7:8] = jnp.zeros((1, per_peer), f32)


def add_records(records, acc, fresh):
    per_peer = records.shape[1]
    highs = acc.shape[0] // 16
    row = lax.broadcasted_iota(jnp.int32, (8, per_peer), 0)
    low_index = lax.broadcasted_iota(jnp.int32, (LOW, per_peer), 0).astype(f32).astype(bf16)
    ids = records[6:7]
    id_high = jnp.floor(ids * (1.0 / LOW))
    id_low = ids - id_high * LOW
    kept = jnp.where(row == 6, 1.0, records)
    high, low = split2(kept)
    pieces = jnp.concatenate([high, low], axis=0).astype(bf16)
    high_b = jnp.broadcast_to(id_high, (16, per_peer)).astype(bf16)
    zero = jnp.zeros_like(pieces)
    lhs = jnp.concatenate(
        [jnp.where(high_b == jnp.asarray(h, bf16), pieces, zero) for h in range(highs)], axis=0
    )
    low_b = jnp.broadcast_to(id_low, (LOW, per_peer)).astype(bf16)
    rhs = jnp.where(low_b == low_index, jnp.ones((), bf16), jnp.zeros((), bf16))
    term = lax.dot_general(lhs, rhs, (((1,), (1,)), ((), ())), preferred_element_type=f32)
    if fresh:
        acc[...] = term
    else:
        acc[...] += term


def forward_kernel(*refs):
    *arrived, out = refs
    for n, chunk in enumerate(arrived):
        out[n] = chunk[1]


def scatter_near_kernel(*refs):
    *arrived, acc = refs
    for n, chunk in enumerate(arrived):
        add_records(chunk[0], acc, n == 0)


def scatter_kernel(first, arrived, boxes, row_a, row_b, left, right, acc):
    highs = acc.shape[0] // 16
    for n in range(arrived.shape[0]):
        add_records(arrived[n], acc, n == 0)
    rows_here, cols_here = boxes.shape[:2]
    for h in range(highs):
        both = acc[16 * h : 16 * h + 16] + first[16 * h : 16 * h + 16]
        block = both[:8] + both[8:]
        for k in range(LOW // SLOT):
            i, j = divmod(h * (LOW // SLOT) + k, cols_here)
            piece = block[:, k * SLOT : (k + 1) * SLOT]
            boxes[i, j] = piece
            if j == 0:
                left[i] = piece
            if j == cols_here - 1:
                right[i] = piece
    even = (lax.axis_index("flow") & 1) == 0
    row_a[...] = jnp.where(even, boxes[rows_here - 1], boxes[0])
    row_b[...] = jnp.where(even, boxes[0], boxes[rows_here - 1])


def edges_kernel(row_a, row_b, left, right, col_a, col_b):
    even_f = (lax.axis_index("flow") & 1) == 0
    even_w = (lax.axis_index("width") & 1) == 0
    rows_here, last = left.shape[0], row_a.shape[0] - 1

    def column(edge, at):
        one, two = row_a[at], row_b[at]
        return [jnp.where(even_f, two, one)] + [edge[i] for i in range(rows_here)] + [
            jnp.where(even_f, one, two)
        ]

    for i, (low, high) in enumerate(zip(column(left, 0), column(right, last))):
        col_a[i] = jnp.where(even_w, high, low)
        col_b[i] = jnp.where(even_w, low, high)


def moments_kernel(offset_hbm, tops_hbm, boxes, out, acc, offset, tops, sems):
    copies = [
        pltpu.make_async_copy(offset_hbm, offset, sems.at[0]),
        pltpu.make_async_copy(tops_hbm, tops, sems.at[1]),
    ]
    for copy in copies:
        copy.start()
    count = boxes.shape[0] // 8
    rows_here = tops.shape[0]

    def line(block):
        return jnp.concatenate([block[i : i + 1] for i in range(rows_here)] * 2, axis=1)

    fields = []
    for f in range(6):
        plane = boxes[pl.ds(f, count, stride=8), :]
        both = jnp.concatenate([plane, pltpu.roll(plane, SLOT - count, 1)], axis=0)
        fields.append(jnp.transpose(both)[:count])
    for copy in copies:
        copy.wait()
    fields = [x + line(offset[f]) if f < 3 else x for f, x in enumerate(fields)]
    index = {t: m for m, t in enumerate(TERMS)}
    chunk = MOMENT_ROWS
    for k in range(count // chunk):
        part = slice(k * chunk, (k + 1) * chunk)
        powers = []
        for f in range(3):
            x = fields[f][part]
            column = [None, x]
            for d in range(2, ORDER + 1):
                column.append(column[-1] * (x * (1.0 / d)))
            powers.append(column)
        spins = [fields[3 + f][part] for f in range(3)]
        for c in range(3):
            for a in range(ORDER + 1):
                lead_a = spins[c] if a == 0 else spins[c] * powers[0][a]
                for b in range(ORDER + 1 - a):
                    lead = lead_a if b == 0 else lead_a * powers[1][b]
                    for n in range(ORDER + 1 - a - b):
                        value = lead if n == 0 else lead * powers[2][n]
                        while value.shape[0] > 8:
                            half = value.shape[0] // 2
                            value = value[:half] + value[half:]
                        at = c * N_TERMS + index[(a, b, n)]
                        if k == 0:
                            acc[8 * at : 8 * at + 8] = value
                        else:
                            acc[8 * at : 8 * at + 8] += value
    acc[8 * COEF : 8 * COEF + 8] = jnp.zeros((8, SLOT), f32)
    total = acc[pl.ds(0, 2 * HALF_ROWS, stride=8), :]
    for s in range(1, 8):
        total = total + acc[pl.ds(s, 2 * HALF_ROWS, stride=8), :]
    total = total + pltpu.roll(total, count, 1)
    lane = lax.broadcasted_iota(jnp.int32, (HALF_ROWS, SLOT), 1)
    out[...] = jnp.where(lane < count, total[:HALF_ROWS], total[HALF_ROWS:])
    last = out[HALF_ROWS - 1 : HALF_ROWS, :]
    ids = line(tops[...].astype(f32))
    out[HALF_ROWS - 1 : HALF_ROWS, :] = jnp.where(lane[:1] < count, last, ids)


def tops_kernel(*refs):
    *shares, out, ready, sems = refs
    shares = [share[n] for share in shares for n in range(share.shape[0])]
    tops_here = out.shape[2]
    base = lax.axis_index("flow") * tops_here
    lane = lax.broadcasted_iota(jnp.int32, (HALF_ROWS, SLOT), 1)
    wanted = (lax.broadcasted_iota(jnp.int32, (tops_here, SLOT), 0) + base).astype(f32)
    half = SLOT // 2
    pairs = [(shares[f], shares[f + 1]) for f in range(0, len(shares), 2)]
    last = slice(HALF_ROWS - 1, HALF_ROWS)
    members = []
    for one, two in pairs:
        ids = jnp.where(lane[:1] < half, pltpu.roll(one[last], half, 1), two[last])
        members.append(jnp.where(wanted == ids, 1.0, 0.0).astype(bf16))
    copies = []
    for n in range(2):
        total = None
        for (one, two), member in zip(pairs, members):
            if n == 0:
                rest = jnp.where(lane < half, one, pltpu.roll(two, half, 1))
            else:
                rest = jnp.where(lane < half, pltpu.roll(one, half, 1), two)
            for _ in range(3):
                piece = rest.astype(bf16)
                rest = rest - piece.astype(f32)
                term = lax.dot_general(
                    piece, member, (((1,), (1,)), ((), ())), preferred_element_type=f32
                )
                total = term if total is None else total + term
        rows = min(HALF_ROWS, COEF - n * HALF_ROWS)
        part = pl.ds(n * HALF_ROWS, rows)
        ready[part, 0, :] = total[:rows]
        copies.append(pltpu.make_async_copy(ready.at[part], out.at[part], sems.at[n]))
        copies[-1].start()
    for copy in copies:
        copy.wait()


def near_kernel(
    codes, center, row_a, row_b, col_a, col_b, out, pad, feat, target, raw, weight, shifts, masks, k_high, k_low, sums, pairs, sem
):
    rows_here, cols_here = center.shape[:2]
    count = rows_here * cols_here
    wide = cols_here + 2
    boxes_all = (rows_here + 2) * wide
    row = rows8()

    listed = pltpu.make_async_copy(codes, pairs, sem)
    listed.start()

    def at8(b):
        return pl.ds(b * 8 if isinstance(b, int) else pl.multiple_of(b * 8, 8), 8)

    def field_of(ref, first, f):
        return ref[pl.ds(first * 8 + f, 8, stride=8), :]

    even_f = (lax.axis_index("flow") & 1) == 0
    even_w = (lax.axis_index("width") & 1) == 0
    for j in range(cols_here):
        for i in range(rows_here):
            pad[at8((i + 1) * wide + 1 + j), :] = center[i, j]
        pad[at8(1 + j), :] = jnp.where(even_f, row_b[j], row_a[j])
        pad[at8((rows_here + 1) * wide + 1 + j), :] = jnp.where(even_f, row_a[j], row_b[j])
    for i in range(rows_here + 2):
        pad[at8(i * wide), :] = jnp.where(even_w, col_b[i], col_a[i])
        pad[at8(i * wide + wide - 1), :] = jnp.where(even_w, col_a[i], col_b[i])
    zeros8 = jnp.zeros((8, SLOT), f32)
    for b in range(boxes_all, pad.shape[0] // 8):
        pad[at8(b), :] = zeros8

    for k in range(9):
        d0, d1 = float(k // 3 - 1), float(k % 3 - 1)
        a_rows = [-d0, -d1, 0.0, -d0, -d1, 0.0, d0 * d0 + d1 * d1, 0.0]
        b_rows = [-2 * d0, -2 * d1, 0.0, -2 * d0, -2 * d1, 0.0, 1.0, 1.0]
        tile_a, tile_b = zeros8, zeros8
        for r in range(8):
            tile_a = jnp.where(row == r, a_rows[r], tile_a)
            tile_b = jnp.where(row == r, b_rows[r], tile_b)
        shifts[k] = jnp.concatenate([tile_a, tile_b], axis=0).astype(bf16)
        turns = jnp.zeros((8, SLOT), f32)
        for r, value in enumerate((d1, d0, d0, d1)):
            turns = jnp.where(row == r, value, turns)
        masks[k] = jnp.concatenate([zeros8 + 1.0, turns] * 2, axis=0).astype(bf16)

    for start in range(0, boxes_all, 8):
        y0, y1, y2, w0, w1, w2 = (field_of(pad, start, f) for f in range(6))
        values = [w0, w1, w2, y1 * w2 - y2 * w1, y2 * w0 - y0 * w2, y0 * w1 - y1 * w0, zeros8, zeros8]
        values += [w2, w2, w1, w0] + [zeros8] * 4
        for f, value in enumerate(values):
            raw[pl.ds(start * 16 + f, 8, stride=16), :] = value
        pad[pl.ds(start * 8 + 7, 8, stride=8), :] = y0 * y0 + y1 * y1 + y2 * y2

    def prepare(at, _):
        y = pad[at8(at), :]
        norm = jnp.broadcast_to(y[7:8], (8, SLOT))
        high, low = split2(y)
        turned = pltpu.roll(low, 3, 0)
        n1, rest = split2(norm)
        n2, rest = split2(rest)
        first = jnp.where(row < 3, -2.0 * high, jnp.where(row < 6, -2.0 * turned, 1.0))
        second = jnp.where(row == 7, n1, first)
        fourth = jnp.where(row == 6, n2, jnp.where(row == 7, rest, 1.0))
        feat[at, 0:16] = jnp.concatenate([first, second], axis=0).astype(bf16)
        feat[at, 16:32] = jnp.concatenate([first, fourth], axis=0).astype(bf16)
        high, low = split2(raw[pl.ds(pl.multiple_of(at * 16, 16), 16), :])
        weight[at] = jnp.concatenate([high, low], axis=0).astype(bf16)
        return 0

    lax.fori_loop(0, boxes_all, prepare, 0, unroll=6)

    const_row = jnp.where((row == 2) | (row == 5) | (row == 7), 0.0, 1.0)

    def place(b):
        i = lax.div(b, cols_here) if cols_here & (cols_here - 1) else b >> (cols_here.bit_length() - 1)
        return i, b - i * cols_here

    def sources(b):
        i, j = place(b)
        corner = i * wide + j
        found = [(4, None, None, corner + wide + 1)]
        for q in range(pairs.shape[0]):
            code = pairs[q, i, j]
            k = jnp.where(code >= 4, code + 1, code)
            r = (k * 11) >> 5
            c = k - 3 * r
            found.append((k, r, c, corner + r * wide + c))
        return found

    def target_stage(b, slot):
        i, j = place(b)
        x = pad[at8((i + 1) * wide + 1 + j), :]
        high, low = split2(x)
        a1, rest = split2(jnp.broadcast_to(x[7:8], (8, SLOT)) + core_sq)
        a2, a3 = split2(rest)
        high3, low3 = pltpu.roll(high, 3, 0), pltpu.roll(low, 3, 0)
        rows = [
            jnp.where(row < 3, high, jnp.where(row < 6, high3, jnp.where(row == 6, a1, a2))),
            jnp.where(row < 3, low, jnp.where(row < 6, low3, jnp.where(row == 6, a3, 1.0))),
            const_row,
            jnp.where(row < 3, high, jnp.where(row < 6, low3, 1.0)),
        ]
        target[slot] = jnp.transpose(jnp.concatenate(rows, axis=0).astype(bf16))

    def kernel_stage(b, slot):
        features = []
        for k, _, _, source in sources(b):
            second = feat[source, 16:32] * shifts[k]
            features.append(jnp.concatenate([feat[source, 0:16], second], axis=0))
        feature = jnp.concatenate(features, axis=1)
        dist = lax.dot_general(
            target[slot], feature, (((1,), (0,)), ((), ())), preferred_element_type=f32
        )
        root = lax.rsqrt(dist)
        kernel = root * root * root
        high = kernel.astype(bf16)
        k_high[slot] = high
        k_low[slot] = (kernel - high.astype(f32)).astype(bf16)

    def field_stage(b, slot):
        tiles = [weight[source] * masks[k] for k, _, _, source in sources(b)]
        lhs = jnp.concatenate(tiles, axis=1)
        dims = (((1,), (1,)), ((), ()))
        main = lax.dot_general(lhs, k_high[slot], dims, preferred_element_type=f32)
        rest = lax.dot_general(lhs[0:16], k_low[slot], dims, preferred_element_type=f32)
        sums[0, at8(b), :] = main[0:8] + main[16:24] + rest[0:8]
        sums[1, at8(b), :] = main[8:16] + main[24:32] + rest[8:16]

    listed.wait()
    slots = k_high.shape[0]
    for u in range(LAG + 1):
        target_stage(u, u)
    for u in range(LAG):
        kernel_stage(u, u)

    def some_boxes(t, _):
        for u in range(slots):
            b = slots * t + u
            kernel_stage(jnp.minimum(b + LAG, count - 1), (u + LAG) % slots)
            field_stage(b, u)
            target_stage(jnp.minimum(b + LAG + 1, count - 1), (u + LAG + 1) % slots)
        return 0

    lax.fori_loop(0, count // slots, some_boxes, 0)

    for i in range(rows_here):
        for j in range(0, cols_here, 8):
            at = (i + 1) * wide + 1 + j
            b = i * cols_here + j
            x0, x1, x2 = (field_of(pad, at, f) for f in range(3))
            scale = -inv_four_pi * field_of(pad, at, 6)
            a0, a1, a2, b0, b1, b2 = (field_of(sums.at[0], b, f) for f in range(6))
            h0, h1, h2, h3 = (field_of(sums.at[1], b, f) for f in range(4))
            out[0, i, j : j + 8, :] = scale * (x1 * a2 - x2 * a1 - (b0 + h0))
            out[1, i, j : j + 8, :] = scale * (x2 * a0 - x0 * a2 - (b1 - h1))
            out[2, i, j : j + 8, :] = scale * (x0 * a1 - x1 * a0 - (b2 + h2 - h3))


def spec(space):
    return pl.BlockSpec(memory_space=space)


def call(kernel, out_shape, spaces, scratch=(), cost=(0, 0), name=None, limit=8, out_space=VMEM):
    many = isinstance(out_shape, (list, tuple))
    return pl.pallas_call(
        kernel,
        out_shape=out_shape,
        in_specs=[spec(s) for s in spaces],
        out_specs=[spec(out_space)] * len(out_shape) if many else spec(out_space),
        scratch_shapes=list(scratch),
        compiler_params=pltpu.CompilerParams(vmem_limit_bytes=limit * 1024 * 1024),
        cost_estimate=pl.CostEstimate(flops=cost[0], bytes_accessed=cost[1], transcendentals=0),
        name=name,
    )


def shape(*dims):
    return jax.ShapeDtypeStruct(dims, f32)


def in_hbm(x):
    return pltpu.with_memory_space_constraint(x, pltpu.HBM)


def swap(axis, step):
    return [(i, i ^ step) for i in range(lax.axis_size(axis))]


def swap_odd(axis):
    odd = range(1, lax.axis_size(axis) - 1, 2)
    return [(i, i + 1) for i in odd] + [(i + 1, i) for i in odd]


def shards(positions, vorticity, dest_slot, send_counts, near_pairs, box_top, box_offset):
    slot_total = positions.shape[1]
    peers = lax.axis_size("width")
    flows = lax.axis_size("flow")
    per_peer = slot_total // peers
    rows_here, cols_here = box_top.shape
    count = rows_here * cols_here
    outgoing = call(
        pack_kernel,
        [shape(2, 8, per_peer)] * (peers // 2),
        [pltpu.HBM] * 4,
        [
            VMEM((3, slot_total), f32),
            VMEM((3, slot_total), f32),
            VMEM((1, slot_total), jnp.int32),
            SMEM((1, peers), jnp.int32),
            pltpu.SemaphoreType.DMA((4,)),
        ],
        name="pack",
    )(
        in_hbm(send_counts),
        in_hbm(positions),
        in_hbm(vorticity),
        in_hbm(dest_slot.reshape(1, slot_total)),
    )
    arrived = [
        lax.ppermute(outgoing[n], "width", swap("width", 2 * n))
        for n in [peers // 4, *(n for n in range(peers // 2 - 1, 0, -1) if n != peers // 4)]
    ]
    arrived.append(outgoing[0])
    passed = call(
        forward_kernel, shape(len(arrived), 8, per_peer), [VMEM] * len(arrived), name="forward"
    )(*arrived)
    passed = lax.ppermute(passed, "width", swap("width", 1))
    part = call(
        scatter_near_kernel,
        shape(slot_total // LOW * 16, LOW),
        [VMEM] * len(arrived),
        cost=(5_000_000_000, 1_000_000),
        name="scatter_near",
    )(*arrived)
    boxes, row_a, row_b, left, right = call(
        scatter_kernel,
        [shape(rows_here, cols_here, 8, SLOT)]
        + [shape(cols_here, 8, SLOT)] * 2
        + [shape(rows_here, 8, SLOT)] * 2,
        [VMEM] * 2,
        [VMEM((slot_total // LOW * 16, LOW), f32)],
        name="scatter",
    )(part, passed)
    row_b = lax.ppermute(row_b, "flow", swap_odd("flow"))
    row_a = lax.ppermute(row_a, "flow", swap("flow", 1))
    local = call(
        moments_kernel,
        shape(HALF_ROWS, SLOT),
        [pltpu.HBM, pltpu.HBM, VMEM],
        [
            VMEM((16 * HALF_ROWS + 8, SLOT), f32),
            VMEM((3, rows_here, cols_here), f32),
            VMEM((rows_here, cols_here), jnp.int32),
            pltpu.SemaphoreType.DMA((2,)),
        ],
        cost=(10_000_000, 1_000_000),
        name="moments",
    )(in_hbm(box_offset), in_hbm(box_top), boxes.reshape(8 * count, SLOT))
    shares = [local[None]]
    for s in range(1, flows):
        shares.append(lax.ppermute(local, "flow", swap("flow", s))[None])
    row_a, row_b, _ = lax.optimization_barrier((row_a, row_b, local))
    col_a, col_b = call(
        edges_kernel, [shape(rows_here + 2, 8, SLOT)] * 2, [VMEM] * 4, name="edges"
    )(row_a, row_b, left, right)
    col_a = lax.ppermute(col_a, "width", swap("width", 1))
    col_b = lax.ppermute(col_b, "width", swap_odd("width"))
    padded = -(-(rows_here + 2) * (cols_here + 2) // 8) * 8
    velocity = call(
        near_kernel,
        shape(3, rows_here, cols_here, SLOT),
        [pltpu.HBM] + [VMEM] * 5,
        [
            VMEM((8 * padded, SLOT), f32),
            VMEM((padded, 32, SLOT), bf16),
            VMEM((UNROLL, SLOT, 32), bf16),
            VMEM((16 * padded, SLOT), f32),
            VMEM((padded, 32, SLOT), bf16),
            VMEM((9, 16, SLOT), bf16),
            VMEM((9, 32, SLOT), bf16),
            VMEM((UNROLL, SLOT, 4 * SLOT), bf16),
            VMEM((UNROLL, SLOT, 4 * SLOT), bf16),
            VMEM((2, 8 * count, SLOT), f32),
            SMEM((near_pairs.shape[2], rows_here, cols_here), jnp.int32),
            pltpu.SemaphoreType.DMA,
        ],
        cost=(5_000_000_000, 2_000_000),
        name="near",
        limit=28,
    )(in_hbm(near_pairs.transpose(2, 0, 1)), boxes, row_a, row_b, col_a, col_b)
    tops_here = TOP // flows
    summed = call(
        tops_kernel,
        shape(COEF, 1, tops_here),
        [VMEM] * len(shares),
        [VMEM((COEF, 1, tops_here), f32), pltpu.SemaphoreType.DMA((2,))],
        name="tops",
        out_space=pltpu.HBM,
    )(*shares)
    return (velocity, summed.transpose(1, 2, 0))


def solution(mesh):
    placed = (
        P(None, ("flow", "width")),
        P(None, ("flow", "width")),
        P(("flow", "width")),
        P(("flow", "width"), None),
        P("flow", "width", None),
        P("flow", "width"),
        P(None, "flow", "width"),
    )
    return jax.shard_map(
        shards,
        mesh=mesh,
        in_specs=placed,
        out_specs=(P(None, "flow", "width", None), P("width", "flow", None)),
        check_vma=False,
    )
```

```python
import functools
import math

import jax
import jax.numpy as jnp
from jax import lax
from jax.experimental import pallas as pl
from jax.experimental.pallas import tpu as pltpu
from jax.sharding import PartitionSpec as P

SLOT = 128
ORDER = 8
TOP = 1024
TERMS = [
    (a, b, s - a - b)
    for s in range(ORDER + 1)
    for a in range(s, -1, -1)
    for b in range(s - a, -1, -1)
]
N_TERMS = len(TERMS)
COEF = 3 * N_TERMS
HALF_ROWS = (COEF + 1) // 2
LAG = 2
MOMENT_ROWS = 16
UNROLL = 32
LOW = 256

core_sq = 0.25
inv_four_pi = 0.07957747154594767
f32 = jnp.float32
bf16 = jnp.bfloat16
VMEM = pltpu.VMEM
SMEM = pltpu.SMEM


def split2(x):
    high = x.astype(bf16).astype(f32)
    return high, x - high


def rows8(x_shape=(8, SLOT)):
    return lax.broadcasted_iota(jnp.int32, x_shape, 0)


def pack_kernel(send_counts, positions, vorticity, dest, *refs):
    *outs, pos, vor, ids, counts, sems = refs
    copies = [
        pltpu.make_async_copy(src, dst, sems.at[n])
        for n, (src, dst) in enumerate(
            [(positions, pos), (vorticity, vor), (dest, ids), (send_counts, counts)]
        )
    ]
    for copy in copies:
        copy.start()
    per_peer = outs[0].shape[2]
    total = pos.shape[1]
    lane = lax.broadcasted_iota(jnp.int32, (1, per_peer), 1)
    me = lax.axis_index("width")
    for copy in copies:
        copy.wait()
    for n, out in enumerate(outs):
        for side in range(2):
            r = me ^ (2 * n + side)
            part = pl.ds(pl.multiple_of(r * per_peer, SLOT), per_peer)
            out[side, 0:3] = pos[:, part]
            out[side, 3:6] = vor[:, part]
            out[side, 6:7] = jnp.where(lane < counts[0, r], ids[:, part], total).astype(f32)
            out[side, 7:8] = jnp.zeros((1, per_peer), f32)


def add_records(records, acc, fresh):
    per_peer = records.shape[1]
    highs = acc.shape[0] // 16
    row = lax.broadcasted_iota(jnp.int32, (8, per_peer), 0)
    low_index = lax.broadcasted_iota(jnp.int32, (LOW, per_peer), 0).astype(f32).astype(bf16)
    ids = records[6:7]
    id_high = jnp.floor(ids * (1.0 / LOW))
    id_low = ids - id_high * LOW
    kept = jnp.where(row == 6, 1.0, records)
    high, low = split2(kept)
    pieces = jnp.concatenate([high, low], axis=0).astype(bf16)
    high_b = jnp.broadcast_to(id_high, (16, per_peer)).astype(bf16)
    zero = jnp.zeros_like(pieces)
    lhs = jnp.concatenate(
        [jnp.where(high_b == jnp.asarray(h, bf16), pieces, zero) for h in range(highs)], axis=0
    )
    low_b = jnp.broadcast_to(id_low, (LOW, per_peer)).astype(bf16)
    rhs = jnp.where(low_b == low_index, jnp.ones((), bf16), jnp.zeros((), bf16))
    term = lax.dot_general(lhs, rhs, (((1,), (1,)), ((), ())), preferred_element_type=f32)
    if fresh:
        acc[...] = term
    else:
        acc[...] += term


def forward_kernel(*refs):
    *arrived, out = refs
    for n, chunk in enumerate(arrived):
        out[n] = chunk[1]


def scatter_near_kernel(*refs):
    *arrived, acc = refs
    for n, chunk in enumerate(arrived):
        add_records(chunk[0], acc, n == 0)


def scatter_kernel(first, arrived, boxes, row_a, row_b, left, right, acc):
    highs = acc.shape[0] // 16
    for n in range(arrived.shape[0]):
        add_records(arrived[n], acc, n == 0)
    rows_here, cols_here = boxes.shape[:2]
    for h in range(highs):
        both = acc[16 * h : 16 * h + 16] + first[16 * h : 16 * h + 16]
        block = both[:8] + both[8:]
        for k in range(LOW // SLOT):
            i, j = divmod(h * (LOW // SLOT) + k, cols_here)
            piece = block[:, k * SLOT : (k + 1) * SLOT]
            boxes[i, j] = piece
            if j == 0:
                left[i] = piece
            if j == cols_here - 1:
                right[i] = piece
    even = (lax.axis_index("flow") & 1) == 0
    row_a[...] = jnp.where(even, boxes[rows_here - 1], boxes[0])
    row_b[...] = jnp.where(even, boxes[0], boxes[rows_here - 1])


def edges_kernel(row_a, row_b, left, right, col_a, col_b):
    even_f = (lax.axis_index("flow") & 1) == 0
    even_w = (lax.axis_index("width") & 1) == 0
    rows_here, last = left.shape[0], row_a.shape[0] - 1

    def column(edge, at):
        one, two = row_a[at], row_b[at]
        return [jnp.where(even_f, two, one)] + [edge[i] for i in range(rows_here)] + [
            jnp.where(even_f, one, two)
        ]

    for i, (low, high) in enumerate(zip(column(left, 0), column(right, last))):
        col_a[i] = jnp.where(even_w, high, low)
        col_b[i] = jnp.where(even_w, low, high)


def moments_kernel(offset_hbm, tops_hbm, boxes, out, acc, offset, tops, sems):
    copies = [
        pltpu.make_async_copy(offset_hbm, offset, sems.at[0]),
        pltpu.make_async_copy(tops_hbm, tops, sems.at[1]),
    ]
    for copy in copies:
        copy.start()
    count = boxes.shape[0] // 8
    rows_here = tops.shape[0]

    def line(block):
        return jnp.concatenate([block[i : i + 1] for i in range(rows_here)] * 2, axis=1)

    fields = []
    for f in range(6):
        plane = boxes[pl.ds(f, count, stride=8), :]
        both = jnp.concatenate([plane, pltpu.roll(plane, SLOT - count, 1)], axis=0)
        fields.append(jnp.transpose(both)[:count])
    for copy in copies:
        copy.wait()
    fields = [x + line(offset[f]) if f < 3 else x for f, x in enumerate(fields)]
    index = {t: m for m, t in enumerate(TERMS)}
    chunk = MOMENT_ROWS
    for k in range(count // chunk):
        part = slice(k * chunk, (k + 1) * chunk)
        powers = []
        for f in range(3):
            x = fields[f][part]
            column = [None, x]
            for d in range(2, ORDER + 1):
                column.append(column[-1] * (x * (1.0 / d)))
            powers.append(column)
        spins = [fields[3 + f][part] for f in range(3)]
        for c in range(3):
            for a in range(ORDER + 1):
                lead_a = spins[c] if a == 0 else spins[c] * powers[0][a]
                for b in range(ORDER + 1 - a):
                    lead = lead_a if b == 0 else lead_a * powers[1][b]
                    for n in range(ORDER + 1 - a - b):
                        value = lead if n == 0 else lead * powers[2][n]
                        while value.shape[0] > 8:
                            half = value.shape[0] // 2
                            value = value[:half] + value[half:]
                        at = c * N_TERMS + index[(a, b, n)]
                        if k == 0:
                            acc[8 * at : 8 * at + 8] = value
                        else:
                            acc[8 * at : 8 * at + 8] += value
    acc[8 * COEF : 8 * COEF + 8] = jnp.zeros((8, SLOT), f32)
    total = acc[pl.ds(0, 2 * HALF_ROWS, stride=8), :]
    for s in range(1, 8):
        total = total + acc[pl.ds(s, 2 * HALF_ROWS, stride=8), :]
    total = total + pltpu.roll(total, count, 1)
    lane = lax.broadcasted_iota(jnp.int32, (HALF_ROWS, SLOT), 1)
    out[...] = jnp.where(lane < count, total[:HALF_ROWS], total[HALF_ROWS:])
    last = out[HALF_ROWS - 1 : HALF_ROWS, :]
    ids = line(tops[...].astype(f32))
    out[HALF_ROWS - 1 : HALF_ROWS, :] = jnp.where(lane[:1] < count, last, ids)


def tops_kernel(*refs):
    *shares, out, ready, sems = refs
    shares = [share[n] for share in shares for n in range(share.shape[0])]
    tops_here = out.shape[2]
    base = lax.axis_index("flow") * tops_here
    lane = lax.broadcasted_iota(jnp.int32, (HALF_ROWS, SLOT), 1)
    wanted = (lax.broadcasted_iota(jnp.int32, (tops_here, SLOT), 0) + base).astype(f32)
    half = SLOT // 2
    pairs = [(shares[f], shares[f + 1]) for f in range(0, len(shares), 2)]
    last = slice(HALF_ROWS - 1, HALF_ROWS)
    members = []
    for one, two in pairs:
        ids = jnp.where(lane[:1] < half, pltpu.roll(one[last], half, 1), two[last])
        members.append(jnp.where(wanted == ids, 1.0, 0.0).astype(bf16))
    copies = []
    for n in range(2):
        total = None
        for (one, two), member in zip(pairs, members):
            if n == 0:
                rest = jnp.where(lane < half, one, pltpu.roll(two, half, 1))
            else:
                rest = jnp.where(lane < half, pltpu.roll(one, half, 1), two)
            for _ in range(2):
                piece = rest.astype(bf16)
                rest = rest - piece.astype(f32)
                term = lax.dot_general(
                    piece, member, (((1,), (1,)), ((), ())), preferred_element_type=f32
                )
                total = term if total is None else total + term
        rows = min(HALF_ROWS, COEF - n * HALF_ROWS)
        part = pl.ds(n * HALF_ROWS, rows)
        ready[part, 0, :] = total[:rows]
        copies.append(pltpu.make_async_copy(ready.at[part], out.at[part], sems.at[n]))
        copies[-1].start()
    for copy in copies:
        copy.wait()


def near_kernel(
    codes, center, row_a, row_b, col_a, col_b, out, pad, feat, target, raw, weight, shifts, masks, k_high, k_low, sums, pairs, sem
):
    rows_here, cols_here = center.shape[:2]
    count = rows_here * cols_here
    wide = cols_here + 2
    boxes_all = (rows_here + 2) * wide
    row = rows8()

    listed = pltpu.make_async_copy(codes, pairs, sem)
    listed.start()

    def at8(b):
        return pl.ds(b * 8 if isinstance(b, int) else pl.multiple_of(b * 8, 8), 8)

    def field_of(ref, first, f):
        return ref[pl.ds(first * 8 + f, 8, stride=8), :]

    even_f = (lax.axis_index("flow") & 1) == 0
    even_w = (lax.axis_index("width") & 1) == 0
    for j in range(cols_here):
        for i in range(rows_here):
            pad[at8((i + 1) * wide + 1 + j), :] = center[i, j]
        pad[at8(1 + j), :] = jnp.where(even_f, row_b[j], row_a[j])
        pad[at8((rows_here + 1) * wide + 1 + j), :] = jnp.where(even_f, row_a[j], row_b[j])
    for i in range(rows_here + 2):
        pad[at8(i * wide), :] = jnp.where(even_w, col_b[i], col_a[i])
        pad[at8(i * wide + wide - 1), :] = jnp.where(even_w, col_a[i], col_b[i])
    zeros8 = jnp.zeros((8, SLOT), f32)
    for b in range(boxes_all, pad.shape[0] // 8):
        pad[at8(b), :] = zeros8

    for k in range(9):
        d0, d1 = float(k // 3 - 1), float(k % 3 - 1)
        a_rows = [-d0, -d1, 0.0, -d0, -d1, 0.0, d0 * d0 + d1 * d1, 0.0]
        b_rows = [-2 * d0, -2 * d1, 0.0, -2 * d0, -2 * d1, 0.0, 1.0, 1.0]
        tile_a, tile_b = zeros8, zeros8
        for r in range(8):
            tile_a = jnp.where(row == r, a_rows[r], tile_a)
            tile_b = jnp.where(row == r, b_rows[r], tile_b)
        shifts[k] = jnp.concatenate([tile_a, tile_b], axis=0).astype(bf16)
        turns = jnp.zeros((8, SLOT), f32)
        for r, value in enumerate((d1, d0, d0, d1)):
            turns = jnp.where(row == r, value, turns)
        masks[k] = jnp.concatenate([zeros8 + 1.0, turns] * 2, axis=0).astype(bf16)

    for start in range(0, boxes_all, 8):
        y0, y1, y2, w0, w1, w2 = (field_of(pad, start, f) for f in range(6))
        values = [w0, w1, w2, y1 * w2 - y2 * w1, y2 * w0 - y0 * w2, y0 * w1 - y1 * w0, zeros8, zeros8]
        values += [w2, w2, w1, w0] + [zeros8] * 4
        for f, value in enumerate(values):
            raw[pl.ds(start * 16 + f, 8, stride=16), :] = value
        pad[pl.ds(start * 8 + 7, 8, stride=8), :] = y0 * y0 + y1 * y1 + y2 * y2

    def prepare(at, _):
        y = pad[at8(at), :]
        norm = jnp.broadcast_to(y[7:8], (8, SLOT))
        high, low = split2(y)
        turned = pltpu.roll(low, 3, 0)
        n1, rest = split2(norm)
        n2, rest = split2(rest)
        first = jnp.where(row < 3, -2.0 * high, jnp.where(row < 6, -2.0 * turned, 1.0))
        second = jnp.where(row == 7, n1, first)
        fourth = jnp.where(row == 6, n2, jnp.where(row == 7, rest, 1.0))
        feat[at, 0:16] = jnp.concatenate([first, second], axis=0).astype(bf16)
        feat[at, 16:32] = jnp.concatenate([first, fourth], axis=0).astype(bf16)
        high, low = split2(raw[pl.ds(pl.multiple_of(at * 16, 16), 16), :])
        weight[at] = jnp.concatenate([high, low], axis=0).astype(bf16)
        return 0

    lax.fori_loop(0, boxes_all, prepare, 0, unroll=6)

    const_row = jnp.where((row == 2) | (row == 5) | (row == 7), 0.0, 1.0)

    def place(b):
        i = lax.div(b, cols_here) if cols_here & (cols_here - 1) else b >> (cols_here.bit_length() - 1)
        return i, b - i * cols_here

    def sources(b):
        i, j = place(b)
        corner = i * wide + j
        found = [(4, None, None, corner + wide + 1)]
        for q in range(pairs.shape[0]):
            code = pairs[q, i, j]
            k = jnp.where(code >= 4, code + 1, code)
            r = (k * 11) >> 5
            c = k - 3 * r
            found.append((k, r, c, corner + r * wide + c))
        return found

    def target_stage(b, slot):
        i, j = place(b)
        x = pad[at8((i + 1) * wide + 1 + j), :]
        high, low = split2(x)
        a1, rest = split2(jnp.broadcast_to(x[7:8], (8, SLOT)) + core_sq)
        a2, a3 = split2(rest)
        high3, low3 = pltpu.roll(high, 3, 0), pltpu.roll(low, 3, 0)
        rows = [
            jnp.where(row < 3, high, jnp.where(row < 6, high3, jnp.where(row == 6, a1, a2))),
            jnp.where(row < 3, low, jnp.where(row < 6, low3, jnp.where(row == 6, a3, 1.0))),
            const_row,
            jnp.where(row < 3, high, jnp.where(row < 6, low3, 1.0)),
        ]
        target[slot] = jnp.transpose(jnp.concatenate(rows, axis=0).astype(bf16))

    def kernel_stage(b, slot):
        features = []
        for k, _, _, source in sources(b):
            second = feat[source, 16:32] * shifts[k]
            features.append(jnp.concatenate([feat[source, 0:16], second], axis=0))
        feature = jnp.concatenate(features, axis=1)
        dist = lax.dot_general(
            target[slot], feature, (((1,), (0,)), ((), ())), preferred_element_type=f32
        )
        root = lax.rsqrt(dist)
        kernel = root * root * root
        high = kernel.astype(bf16)
        k_high[slot] = high
        k_low[slot] = (kernel - high.astype(f32)).astype(bf16)

    def field_stage(b, slot):
        tiles = [weight[source] * masks[k] for k, _, _, source in sources(b)]
        lhs = jnp.concatenate(tiles, axis=1)
        dims = (((1,), (1,)), ((), ()))
        main = lax.dot_general(lhs, k_high[slot], dims, preferred_element_type=f32)
        rest = lax.dot_general(lhs[0:16], k_low[slot], dims, preferred_element_type=f32)
        sums[0, at8(b), :] = main[0:8] + main[16:24] + rest[0:8]
        sums[1, at8(b), :] = main[8:16] + main[24:32] + rest[8:16]

    listed.wait()
    slots = k_high.shape[0]
    for u in range(LAG + 1):
        target_stage(u, u)
    for u in range(LAG):
        kernel_stage(u, u)

    def some_boxes(t, _):
        for u in range(slots):
            b = slots * t + u
            kernel_stage(jnp.minimum(b + LAG, count - 1), (u + LAG) % slots)
            field_stage(b, u)
            target_stage(jnp.minimum(b + LAG + 1, count - 1), (u + LAG + 1) % slots)
        return 0

    lax.fori_loop(0, count // slots, some_boxes, 0)

    for i in range(rows_here):
        for j in range(0, cols_here, 8):
            at = (i + 1) * wide + 1 + j
            b = i * cols_here + j
            x0, x1, x2 = (field_of(pad, at, f) for f in range(3))
            scale = -inv_four_pi * field_of(pad, at, 6)
            a0, a1, a2, b0, b1, b2 = (field_of(sums.at[0], b, f) for f in range(6))
            h0, h1, h2, h3 = (field_of(sums.at[1], b, f) for f in range(4))
            out[0, i, j : j + 8, :] = scale * (x1 * a2 - x2 * a1 - (b0 + h0))
            out[1, i, j : j + 8, :] = scale * (x2 * a0 - x0 * a2 - (b1 - h1))
            out[2, i, j : j + 8, :] = scale * (x0 * a1 - x1 * a0 - (b2 + h2 - h3))


def spec(space):
    return pl.BlockSpec(memory_space=space)


def call(kernel, out_shape, spaces, scratch=(), cost=(0, 0), name=None, limit=8, out_space=VMEM):
    many = isinstance(out_shape, (list, tuple))
    return pl.pallas_call(
        kernel,
        out_shape=out_shape,
        in_specs=[spec(s) for s in spaces],
        out_specs=[spec(out_space)] * len(out_shape) if many else spec(out_space),
        scratch_shapes=list(scratch),
        compiler_params=pltpu.CompilerParams(vmem_limit_bytes=limit * 1024 * 1024),
        cost_estimate=pl.CostEstimate(flops=cost[0], bytes_accessed=cost[1], transcendentals=0),
        name=name,
    )


def shape(*dims):
    return jax.ShapeDtypeStruct(dims, f32)


def in_hbm(x):
    return pltpu.with_memory_space_constraint(x, pltpu.HBM)


def swap(axis, step):
    return [(i, i ^ step) for i in range(lax.axis_size(axis))]


def swap_odd(axis):
    odd = range(1, lax.axis_size(axis) - 1, 2)
    return [(i, i + 1) for i in odd] + [(i + 1, i) for i in odd]


def shards(positions, vorticity, dest_slot, send_counts, near_pairs, box_top, box_offset):
    slot_total = positions.shape[1]
    peers = lax.axis_size("width")
    flows = lax.axis_size("flow")
    per_peer = slot_total // peers
    rows_here, cols_here = box_top.shape
    count = rows_here * cols_here
    outgoing = call(
        pack_kernel,
        [shape(2, 8, per_peer)] * (peers // 2),
        [pltpu.HBM] * 4,
        [
            VMEM((3, slot_total), f32),
            VMEM((3, slot_total), f32),
            VMEM((1, slot_total), jnp.int32),
            SMEM((1, peers), jnp.int32),
            pltpu.SemaphoreType.DMA((4,)),
        ],
        name="pack",
    )(
        in_hbm(send_counts),
        in_hbm(positions),
        in_hbm(vorticity),
        in_hbm(dest_slot.reshape(1, slot_total)),
    )
    arrived = [
        lax.ppermute(outgoing[n], "width", swap("width", 2 * n))
        for n in range(peers // 2 - 1, 0, -1)
    ]
    arrived.append(outgoing[0])
    passed = call(
        forward_kernel, shape(len(arrived), 8, per_peer), [VMEM] * len(arrived), name="forward"
    )(*arrived)
    passed = lax.ppermute(passed, "width", swap("width", 1))
    part = call(
        scatter_near_kernel,
        shape(slot_total // LOW * 16, LOW),
        [VMEM] * len(arrived),
        cost=(5_000_000_000, 1_000_000),
        name="scatter_near",
    )(*arrived)
    boxes, row_a, row_b, left, right = call(
        scatter_kernel,
        [shape(rows_here, cols_here, 8, SLOT)]
        + [shape(cols_here, 8, SLOT)] * 2
        + [shape(rows_here, 8, SLOT)] * 2,
        [VMEM] * 2,
        [VMEM((slot_total // LOW * 16, LOW), f32)],
        name="scatter",
    )(part, passed)
    row_b = lax.ppermute(row_b, "flow", swap_odd("flow"))
    row_a = lax.ppermute(row_a, "flow", swap("flow", 1))
    local = call(
        moments_kernel,
        shape(HALF_ROWS, SLOT),
        [pltpu.HBM, pltpu.HBM, VMEM],
        [
            VMEM((16 * HALF_ROWS + 8, SLOT), f32),
            VMEM((3, rows_here, cols_here), f32),
            VMEM((rows_here, cols_here), jnp.int32),
            pltpu.SemaphoreType.DMA((2,)),
        ],
        cost=(10_000_000, 1_000_000),
        name="moments",
    )(in_hbm(box_offset), in_hbm(box_top), boxes.reshape(8 * count, SLOT))
    shares = [local[None]]
    for s in range(1, flows):
        shares.append(lax.ppermute(local, "flow", swap("flow", s))[None])
    row_a, row_b, _ = lax.optimization_barrier((row_a, row_b, local))
    col_a, col_b = call(
        edges_kernel, [shape(rows_here + 2, 8, SLOT)] * 2, [VMEM] * 4, name="edges"
    )(row_a, row_b, left, right)
    col_a = lax.ppermute(col_a, "width", swap("width", 1))
    col_b = lax.ppermute(col_b, "width", swap_odd("width"))
    padded = -(-(rows_here + 2) * (cols_here + 2) // 8) * 8
    velocity = call(
        near_kernel,
        shape(3, rows_here, cols_here, SLOT),
        [pltpu.HBM] + [VMEM] * 5,
        [
            VMEM((8 * padded, SLOT), f32),
            VMEM((padded, 32, SLOT), bf16),
            VMEM((UNROLL, SLOT, 32), bf16),
            VMEM((16 * padded, SLOT), f32),
            VMEM((padded, 32, SLOT), bf16),
            VMEM((9, 16, SLOT), bf16),
            VMEM((9, 32, SLOT), bf16),
            VMEM((UNROLL, SLOT, 4 * SLOT), bf16),
            VMEM((UNROLL, SLOT, 4 * SLOT), bf16),
            VMEM((2, 8 * count, SLOT), f32),
            SMEM((near_pairs.shape[2], rows_here, cols_here), jnp.int32),
            pltpu.SemaphoreType.DMA,
        ],
        cost=(5_000_000_000, 2_000_000),
        name="near",
        limit=28,
    )(in_hbm(near_pairs.transpose(2, 0, 1)), boxes, row_a, row_b, col_a, col_b)
    tops_here = TOP // flows
    summed = call(
        tops_kernel,
        shape(COEF, 1, tops_here),
        [VMEM] * len(shares),
        [VMEM((COEF, 1, tops_here), f32), pltpu.SemaphoreType.DMA((2,))],
        name="tops",
        out_space=pltpu.HBM,
    )(*shares)
    return (velocity, summed.transpose(1, 2, 0))


def solution(mesh):
    placed = (
        P(None, ("flow", "width")),
        P(None, ("flow", "width")),
        P(("flow", "width")),
        P(("flow", "width"), None),
        P("flow", "width", None),
        P("flow", "width"),
        P(None, "flow", "width"),
    )
    return jax.shard_map(
        shards,
        mesh=mesh,
        in_specs=placed,
        out_specs=(P(None, "flow", "width", None), P("width", "flow", None)),
        check_vma=False,
    )
```
